32 devices in a mesh: groups: 1, ctx: 16 (over z, y, x), tp: 2 (over core).
Axes of the slice: x: 2, y: 2, z: 4, core: 2. Of those that a mesh axis runs over, the one named last changes fastest.
Arguments:
- queries: bfloat16 [4, 32, 64, 128], P('groups', 'ctx', 'tp'), may hold values from -100 to 100
- cand_keys: bfloat16 [4, 32, 8, 128], P('groups', 'ctx', 'tp'), may hold values from -4 to 4
- candidate_values: bfloat16 [4, 32, 8, 128], P('groups', 'ctx', 'tp'), may hold values from -5 to 5
- cached_prompt_keys: bfloat16 [256, 128, 8, 128], P(('groups', 'ctx'), None, 'tp'), may hold values from -4 to 4
- cached_prompt_values: bfloat16 [256, 128, 8, 128], P(('groups', 'ctx'), None, 'tp'), may hold values from -5 to 5
- block_lists: int32 [4, 128], P('groups'), may hold values from 0 to 255, as said below
- out_weight: bfloat16 [8192, 8192], P('tp', 'ctx'), may hold values from -0.0625 to 0.0625
Outputs:
- verified: bfloat16 [4, 32, 8192], P('groups', 'tp', 'ctx')
The draws below stay inside these ranges and needn't reach their ends.
Inputs may be any that keep to these rules, and one draw needn't show every extreme that they name: `block_lists`: each row holds 128 distinct block numbers in increasing order; among blocks 16 * c to 16 * (c + 1) - 1 a row has at most 16 entries, exactly 16 for some c in every row; all rows together have at most 40 entries in one such range, exactly 40 in some.
All inputs are finite; a program needn't handle non-finite values.
Results may differ from the reference program's by a relative error of at most 0.022.
Values may be sent and summed in bfloat16 or wider, within the bound.
A program may use at most 128 MiB of HBM per device.

```python
import jax
import jax.numpy as jnp
from jax import lax

D = 8192
QUERY_HEADS = 64
KEY_VALUE_HEADS = 8
HEAD_WIDTH = 128
PROMPT_BLOCK = 128
READ_BLOCKS = 128
CANDIDATE_COUNT = 4
BLK_DEV = 16
PROMPT_BLOCKS = 256
CANDIDATE_LENGTH = 32


def paired_draw(key):
    base = jax.random.fold_in(key, 7)
    key_one, random_key_second = jax.random.split(base, 2)
    candidate_own_keys = jnp.clip(jax.random.normal(random_key_second, (CANDIDATE_COUNT, CANDIDATE_LENGTH, KEY_VALUE_HEADS, HEAD_WIDTH), jnp.float32), -4.0, 4.0)
    query_matrix = jnp.clip(jax.random.normal(key_one, (CANDIDATE_COUNT, CANDIDATE_LENGTH, QUERY_HEADS, HEAD_WIDTH), jnp.float32), -4.0, 4.0)
    return (query_matrix, candidate_own_keys)


def draw_queries(key, part):
    return paired_draw(key)[0].astype(jnp.bfloat16)


def draw_cand_keys(key, part):
    return paired_draw(key)[1].astype(jnp.bfloat16)


def draw_block_lists(key, part):
    ranges = PROMPT_BLOCKS // BLK_DEV
    most = min(BLK_DEV, 4 * READ_BLOCKS // ranges)
    second = most // 2
    base = jax.random.fold_in(key, 11)
    busiest = jax.random.permutation(jax.random.fold_in(base, 1), ranges)[:CANDIDATE_COUNT]

    def candidate(index):
        own_key = jax.random.fold_in(base, 100 + index)
        key_one, random_key_second = jax.random.split(own_key)
        device = jnp.arange(ranges)
        is_busy = device == busiest[index]
        forced = (device == busiest[0]) & (index > 0)
        remaining = READ_BLOCKS - most - jnp.where(index > 0, second, 0)
        scores = jax.random.permutation(key_one, ranges * second).reshape(ranges, second)
        eligible = jnp.logical_not(is_busy | forced)
        scores = jnp.where(eligible[:, None], scores, ranges * second + 1)
        ranking = jnp.argsort(jnp.argsort(scores.reshape(-1))).reshape(ranges, second)
        chosen = ranking < remaining
        counts = jnp.where(is_busy, most, jnp.where(forced, second, jnp.sum(chosen.astype(jnp.int32), axis=1)))
        orders = jax.vmap(lambda sub: jax.random.permutation(sub, BLK_DEV))(jax.random.split(random_key_second, ranges))[:, :most]
        blocks = device[:, None] * BLK_DEV + orders
        slot = jnp.arange(most)
        marked = jnp.where(slot[None, :] < counts[:, None], blocks, PROMPT_BLOCKS + 1)
        return jnp.sort(marked.reshape(-1))[:READ_BLOCKS].astype(jnp.int32)
    return jax.vmap(candidate)(jnp.arange(CANDIDATE_COUNT))


def block_levels(rng, dims, pieces, smallest, largest):
    gain, own = 1.0, jax.random.fold_in(rng, 6)
    for dim, blocks in pieces:
        heights = jnp.exp(jax.random.uniform(jax.random.fold_in(own, dim), (blocks,), jnp.float32, smallest / len(pieces), largest / len(pieces)))
        gain = gain * jnp.repeat(heights, dims[dim] // blocks).reshape([-1 if axis == dim else 1 for axis in range(len(dims))])
    return gain


def scatter_about(key, extent, spread, limit, pieces=(), kind=jnp.bfloat16):
    result = spread * jax.random.normal(key, extent, jnp.float32)
    if pieces:
        result = result * block_levels(key, extent, pieces, -0.22, 0.18)
    return jnp.clip(result, -limit, limit).astype(kind)


def setup_inputs(seed: int = 0, part: int = 0) -> dict:
    streams_of = jax.random.split(jax.random.key(seed), 8)
    own_keys = jax.random.split(jax.random.fold_in(streams_of[7], part), 8)
    queries = draw_queries(jax.random.fold_in(jax.random.fold_in(streams_of[7], part), 71), part)
    cand_keys = draw_cand_keys(jax.random.fold_in(jax.random.fold_in(streams_of[7], part), 71), part)
    candidate_values = scatter_about(own_keys[2], (CANDIDATE_COUNT, CANDIDATE_LENGTH, KEY_VALUE_HEADS, HEAD_WIDTH), 1.0, 5.0, ((1, 16), (2, 2)))
    cached_prompt_keys = scatter_about(own_keys[3], (PROMPT_BLOCKS, PROMPT_BLOCK, KEY_VALUE_HEADS, HEAD_WIDTH), 1.0, 4.0, ((0, 16), (2, 2)))
    cached_prompt_values = scatter_about(own_keys[4], (PROMPT_BLOCKS, PROMPT_BLOCK, KEY_VALUE_HEADS, HEAD_WIDTH), 1.0, 5.0, ((0, 16), (2, 2)))
    block_lists = draw_block_lists(jax.random.fold_in(jax.random.fold_in(streams_of[7], part), 71), part)
    out_weight = scatter_about(streams_of[6], (QUERY_HEADS * HEAD_WIDTH, D), (QUERY_HEADS * HEAD_WIDTH) ** -0.5, 0.0625, ((0, 2), (1, 16)))
    return dict(queries=queries, cand_keys=cand_keys, candidate_values=candidate_values, cached_prompt_keys=cached_prompt_keys, cached_prompt_values=cached_prompt_values, block_lists=block_lists, out_weight=out_weight)


def reference(queries, cand_keys, candidate_values, cached_prompt_keys, cached_prompt_values, block_lists, out_weight):
    query_group_width = QUERY_HEADS // KEY_VALUE_HEADS
    factor = HEAD_WIDTH ** -0.5
    position = jnp.arange(CANDIDATE_LENGTH)
    causal = position[None, :] <= position[:, None]
    visible = jnp.concatenate([jnp.ones((CANDIDATE_LENGTH, READ_BLOCKS * PROMPT_BLOCK), dtype=bool), causal], axis=1)

    def candidate(inputs):
        query_matrix, candidate_own_keys, own_values, listed_blocks = inputs
        gathered_keys = jnp.take(cached_prompt_keys, listed_blocks, axis=0).reshape(READ_BLOCKS * PROMPT_BLOCK, KEY_VALUE_HEADS, HEAD_WIDTH)
        gathered_values = jnp.take(cached_prompt_values, listed_blocks, axis=0).reshape(READ_BLOCKS * PROMPT_BLOCK, KEY_VALUE_HEADS, HEAD_WIDTH)
        all_keys = jnp.concatenate([gathered_keys, candidate_own_keys], axis=0)
        all_values = jnp.concatenate([gathered_values, own_values], axis=0)
        grouped_queries = query_matrix.reshape(CANDIDATE_LENGTH, KEY_VALUE_HEADS, query_group_width, HEAD_WIDTH)

        def kv_head(parts):
            head_queries, head_keys, head_values = parts
            scores = jnp.einsum('ngd,md->gnm', head_queries.astype(jnp.float32), head_keys.astype(jnp.float32)) * factor
            scores = jnp.where(visible[None], scores, -1e30)
            maxima = jnp.max(scores, axis=-1, keepdims=True)
            expon = jnp.where(visible[None], jnp.exp(scores - maxima), 0.0)
            denominator = jnp.sum(expon, axis=-1)
            rounded = lax.optimization_barrier(expon.astype(jnp.bfloat16)).astype(jnp.float32)
            numerator = jnp.einsum('gnm,md->ngd', rounded, head_values.astype(jnp.float32))
            return numerator / jnp.transpose(denominator)[:, :, None]

        heads_out = lax.map(kv_head, (jnp.transpose(grouped_queries, (1, 0, 2, 3)), jnp.transpose(all_keys, (1, 0, 2)), jnp.transpose(all_values, (1, 0, 2))))
        return jnp.transpose(heads_out, (1, 0, 2, 3)).reshape(CANDIDATE_LENGTH, QUERY_HEADS * HEAD_WIDTH).astype(jnp.bfloat16)

    attention = lax.map(candidate, (queries, cand_keys, candidate_values, block_lists))
    product = jnp.dot(attention.reshape(CANDIDATE_COUNT * CANDIDATE_LENGTH, QUERY_HEADS * HEAD_WIDTH), out_weight, preferred_element_type=jnp.float32)
    return product.astype(jnp.bfloat16).reshape(CANDIDATE_COUNT, CANDIDATE_LENGTH, D)
```

```python
import functools
import math

import jax
import jax.numpy as jnp
from jax import lax
from jax.experimental import pallas as pl
from jax.experimental.pallas import tpu as pltpu
from jax.sharding import PartitionSpec as P

NEGATIVE = -1e30
MESH = pl.DeviceIdType.MESH
F32, BF16 = jnp.float32, jnp.bfloat16


class Place:
    def __init__(self, ranges):
        self.me = lax.axis_index("ctx")
        self.depth = ranges // 4
        self.x, self.y, self.z = self.me % 2, (self.me // 2) % 2, self.me // 4
        self.beside_x = self.at(self.z, self.y, 1 - self.x)
        self.beside_y = self.at(self.z, 1 - self.y, self.x)

    def at(self, z, y, x):
        return z * 4 + y * 2 + x

    def shifted(self, d):
        return (self.z + d + self.depth) % self.depth

    def line(self, d):
        return self.at(self.shifted(d), self.y, self.x)


def greet(place, with_tp):
    barrier = pltpu.get_barrier_semaphore()
    others = [place.line(d) for d in range(1, place.depth)]
    for other in others + [place.beside_x, place.beside_y]:
        pl.semaphore_signal(barrier, inc=1, device_id={"ctx": other}, device_id_type=MESH)
    if with_tp:
        pl.semaphore_signal(
            barrier, inc=1, device_id={"tp": 1 - lax.axis_index("tp")}, device_id_type=MESH
        )
    pl.semaphore_wait(barrier, place.depth + 1 + int(with_tp))


def near_first(depth):
    order = []
    for step in range(1, depth // 2 + 1):
        order += [step] + ([depth - step] if depth - step != step else [])
    return order


def merge(pieces, combos, per, scale):
    full = combos * per
    stats = [load(full, per).astype(F32) for load in pieces]
    peak = functools.reduce(jnp.maximum, stats)
    low = lax.broadcasted_iota(jnp.int32, (per, 128), 1) < 64
    scales = [jnp.exp2((jnp.where(low, s - peak, 0.0)) * scale) for s in stats]
    total = sum(pltpu.roll(w, 64, 1) * s for w, s in zip(scales, stats))
    sums = []
    for c in range(combos):
        sums.append(
            sum(
                load(c * per, per).astype(F32) * w[:, c : c + 1]
                for load, w in zip(pieces, scales)
            )
        )
    return sums, jnp.where(low, peak, total), total


class Gather:
    def __init__(self, place, buf, send, recv):
        self.place, self.buf, self.send, self.recv = place, buf, send, recv
        self.sent = []
        self.z_of = [place.shifted(-d) for d in range(place.depth)]

    def copy(self, kind, d, half, owner, target):
        return pltpu.make_async_remote_copy(
            src_ref=self.buf.at[owner, half],
            dst_ref=self.buf.at[owner, half],
            send_sem=self.send.at[kind, d, half],
            recv_sem=self.recv.at[kind, d, half],
            device_id={"ctx": target},
            device_id_type=MESH,
        )

    def go(self, *what):
        one = self.copy(*what)
        one.start()
        self.sent.append(one)

    def begin(self, half):
        place = self.place
        self.spread(0, half)
        for d in near_first(place.depth):
            self.go(0, d, half, place.me, place.line(d))

    def spread(self, d, half):
        place = self.place
        owner = place.at(self.z_of[d], place.y, place.x)
        if d:
            self.copy(0, d, half, owner, place.me).wait_recv()
        self.go(1, d, half, owner, place.beside_x)
        self.go(2, d, half, owner, place.beside_y)

    def relay(self, d, half):
        place = self.place
        if half == 0:
            from_x = place.at(self.z_of[d], place.y, 1 - place.x)
            self.copy(1, d, half, from_x, place.me).wait_recv()
            self.go(3, d, half, from_x, place.beside_y)
        else:
            from_y = place.at(self.z_of[d], 1 - place.y, place.x)
            self.copy(2, d, half, from_y, place.me).wait_recv()
            self.go(3, d, half, from_y, place.beside_x)

    def settle(self, half):
        place = self.place
        for d in range(place.depth):
            from_x = place.at(self.z_of[d], place.y, 1 - place.x)
            from_y = place.at(self.z_of[d], 1 - place.y, place.x)
            if half == 0:
                self.copy(2, d, half, from_y, place.me).wait_recv()
            else:
                self.copy(1, d, half, from_x, place.me).wait_recv()
            across = place.at(self.z_of[d], 1 - place.y, 1 - place.x)
            self.copy(3, d, half, across, place.me).wait_recv()

    def finish(self):
        for one in self.sent:
            one.wait_send()


def run_all(steps):
    for step in steps:
        step()


def weave(first, second):
    keyed = [((i + 0.5) / len(first), 0, i, step) for i, step in enumerate(first)]
    keyed += [((i + 0.5) / len(second), 1, i, step) for i, step in enumerate(second)]
    return [item[3] for item in sorted(keyed, key=lambda item: item[:3])]


def fused_kernel(
    ranges,
    sizes,
    lists_smem,
    lists_ref,
    q_ref,
    own_k_ref,
    own_v_ref,
    k_ref,
    v_ref,
    weight_ref,
    out_ref,
    everyone,
    raw,
    wide,
    heads,
    plan,
    queries,
    own_blocks,
    scores,
    run,
    acc,
    peaks,
    own_sums,
    own_acc,
    parts_ref,
    from_diag,
    from_x,
    from_y,
    from_line,
    to_diag,
    to_line,
    gathered,
    ordered,
    weight,
    total,
    away,
    arrived,
    lines,
    in_sems,
    ask_send,
    ask_recv,
    red_send,
    red_recv,
    send,
    recv,
    tp_sems,
):
    cands, toks, kv, group, head, tile_owners, slots = sizes
    place = Place(ranges)
    depth = place.depth
    per = toks * group
    pair = kv // 2
    combos = pair * cands
    scale = head ** (-0.5) * math.log2(math.e)
    rows = tile_owners * per
    blocks, block_tokens = raw.shape[1], raw.shape[2] // kv
    sources = (k_ref, v_ref)
    fetches = [pltpu.make_async_copy(sources[n], raw.at[n], in_sems.at[n]) for n in range(2)]
    for fetch in fetches:
        fetch.start()
    weight_fetch = pltpu.make_async_copy(weight_ref, weight, in_sems.at[2])
    weight_fetch.start()
    for half in range(2):
        everyone[place.me, half] = q_ref[:, :, half * pair * group : (half + 1) * pair * group, :]
    greet(place, True)

    ask = Gather(place, everyone, ask_send, ask_recv)
    near = near_first(depth)
    ask.begin(0)
    ask.begin(1)

    lowest = place.me * blocks
    listed = lists_smem.shape[1]
    below, count, start = [], [], [jnp.int32(0)]
    for j in range(cands):
        line = lists_ref[j : j + 1, :]
        below.append(jnp.sum((line < lowest).astype(jnp.int32)))
        count.append(jnp.sum((line < lowest + blocks).astype(jnp.int32)) - below[j])
        start.append(jnp.minimum(start[j] + (count[j] + 1) // 2, slots))

    def plan_slot(i, carry):
        cand, begun, under, many = jnp.int32(0), jnp.int32(0), below[0], count[0]
        for j in range(1, cands):
            here = i >= start[j]
            cand = jnp.where(here, j, cand)
            begun = jnp.where(here, start[j], begun)
            under = jnp.where(here, below[j], under)
            many = jnp.where(here, count[j], many)
        offset = 2 * (i - begun)
        plan[0, i] = cand
        for n in range(2):
            entry = jnp.minimum(under + offset + n, listed - 1)
            block = lists_smem[cand, entry] - lowest
            plan[1 + n, i] = jnp.minimum(jnp.maximum(block, 0), blocks - 1)
            plan[3 + n, i] = (offset + n < many).astype(jnp.int32)
        plan[5, i] = (offset == 0).astype(jnp.int32)
        return carry

    lax.fori_loop(0, slots, plan_slot, 0)

    def sort_heads(n, first, last):
        def one(b, carry):
            wide[...] = raw[n, b].astype(F32)
            for h in range(kv):
                heads[n, h, b] = wide[pl.ds(h, block_tokens, stride=kv), :].astype(BF16)
            return carry

        lax.fori_loop(first, last, one, 0)

    key_row = lax.broadcasted_iota(jnp.int32, (block_tokens, head), 0)

    def own_rows():
        for n, ref in enumerate((own_k_ref, own_v_ref)):
            mine = [ref[j].astype(F32) for j in range(cands)]
            for h in range(kv):
                block = jnp.zeros((block_tokens, head), F32)
                for j in range(cands):
                    for t in range(toks):
                        block = jnp.where(
                            key_row == j * toks + t, mine[j][t, h : h + 1, :], block
                        )
                own_blocks[n, h] = block.astype(BF16)

    def sort_step(n, part):
        def step():
            if part == 0:
                fetches[n].wait()
            sort_heads(n, part * (blocks // 4), (part + 1) * (blocks // 4))

        return step

    def ask_steps(gather):
        steps = []
        pieces = [(d, half) for half in range(2) for d in [0] + near]
        spreads = [piece for piece in pieces if piece[0]]
        for i, piece in enumerate(pieces):
            ahead = spreads[2 * i : 2 * i + 2] if i == 0 else spreads[i + 1 : i + 2]
            for other in ahead:
                steps.append(functools.partial(gather.spread, *other))
            steps.append(functools.partial(gather.relay, *piece))
        return steps

    local = [sort_step(0, part) for part in range(4)] + [own_rows]
    local += [sort_step(1, part) for part in range(4)]
    run_all(weave(local, ask_steps(ask)))

    nt = (((1,), (1,)), ((), ()))
    row = lax.broadcasted_iota(jnp.int32, (rows, block_tokens), 0)
    lane = lax.broadcasted_iota(jnp.int32, (rows, block_tokens), 1)
    unroll = 2

    def attend(half, tile, between):
        owners = pl.ds(tile * tile_owners, tile_owners)
        query_pos = tile * tile_owners * toks + row // group

        def own_seen(j):
            t = lane - j * toks
            return (t >= 0) & (t < toks) & (place.me * toks + t <= query_pos)

        for hh in range(pair):
            run[hh, 0] = jnp.full((rows, block_tokens), NEGATIVE, F32)
            acc[hh, 0] = jnp.zeros((rows, head), F32)
            for j in range(cands):
                q = everyone[owners, half, j, :, hh * group : (hh + 1) * group, :].astype(F32)
                queries[hh, j] = q.reshape(rows, head).astype(BF16)

        def first_pass(it, carry):
            for u in range(unroll):
                i = it * unroll + u
                cand, fresh = plan[0, i], plan[5, i] > 0
                for hh in range(pair):
                    h = half * pair + hh
                    keys = jnp.concatenate(
                        [heads[0, h, plan[1, i]], heads[0, h, plan[2, i]]], axis=0
                    )
                    s = lax.dot_general(queries[hh, cand], keys, nt, preferred_element_type=F32)
                    top = jnp.where(fresh, NEGATIVE, run[hh, i])
                    for n in range(2):
                        one = s[:, n * block_tokens : (n + 1) * block_tokens]
                        one = jnp.where(plan[3 + n, i] > 0, one, NEGATIVE)
                        scores[hh, i, n] = one
                        top = jnp.maximum(top, one)
                    run[hh, i + 1] = top
            return carry

        lax.fori_loop(0, slots // unroll, first_pass, 0)
        between[0]()
        for hh in range(pair):
            h = half * pair + hh
            for j in range(cands):
                seen = own_seen(j)
                own = lax.dot_general(
                    queries[hh, j], own_blocks[0, h], nt, preferred_element_type=F32
                )
                own = jnp.where(seen, own, NEGATIVE)
                top = jnp.where(count[j] > 0, run[hh, start[j + 1]], NEGATIVE)
                top = jnp.maximum(top, own)
                peak = jnp.max(top, axis=1, keepdims=True).astype(BF16).astype(F32)
                p = jnp.where(seen, jnp.exp2((own - peak) * scale), 0.0)
                own_sums[hh, j] = p
                own_acc[hh, j] = jnp.dot(
                    p.astype(BF16), own_blocks[1, h], preferred_element_type=F32
                )
                peaks[hh, j] = jnp.broadcast_to(peak, (rows, block_tokens))

        def second_pass(it, carry):
            for u in range(unroll):
                i = it * unroll + u
                cand, fresh = plan[0, i], plan[5, i] > 0
                for hh in range(pair):
                    h = half * pair + hh
                    peak = peaks[hh, cand]
                    p = [jnp.exp2((scores[hh, i, n] - peak) * scale) for n in range(2)]
                    run[hh, i + 1] = jnp.where(fresh, 0.0, run[hh, i]) + (p[0] + p[1])
                    values = jnp.concatenate(
                        [heads[1, h, plan[1, i]], heads[1, h, plan[2, i]]], axis=0
                    )
                    weights = jnp.concatenate([one.astype(BF16) for one in p], axis=1)
                    acc[hh, i + 1] = jnp.where(fresh, 0.0, acc[hh, i]) + jnp.dot(
                        weights, values, preferred_element_type=F32
                    )
            return carry

        lax.fori_loop(0, slots // unroll, second_pass, 0)
        between[1]()
        lanes = lax.broadcasted_iota(jnp.int32, (rows, 128), 1)
        stats = jnp.zeros((rows, 128), F32)
        for hh in range(pair):
            for j in range(cands):
                combo = hh * cands + j
                last, some = start[j + 1], count[j] > 0
                sums = jnp.where(some, run[hh, last], 0.0) + own_sums[hh, j]
                found = jnp.where(some, acc[hh, last], 0.0) + own_acc[hh, j]
                stats = jnp.where(lanes == combo, peaks[hh, j], stats)
                stats = jnp.where(
                    lanes == 64 + combo, jnp.sum(sums, axis=1, keepdims=True), stats
                )
                parts_ref[owners, half, combo * per : (combo + 1) * per, :] = found.reshape(
                    tile_owners, per, head
                ).astype(BF16)
        parts_ref[owners, half, combos * per : (combos + 1) * per, :] = stats.reshape(
            tile_owners, per, 128
        ).astype(BF16)

    sent = []

    def copy(kind, d, half, src, dst, target):
        return pltpu.make_async_remote_copy(
            src_ref=src,
            dst_ref=dst.at[d, half],
            send_sem=red_send.at[kind, d, half],
            recv_sem=red_recv.at[kind, d, half],
            device_id={"ctx": target},
            device_id_type=MESH,
        )

    def go(*what):
        one = copy(*what)
        one.start()
        sent.append(one)

    def arrive(kind, d, half, dst):
        copy(kind, d, half, dst.at[d, half], dst, place.me).wait_recv()

    def owner(d, flip_y, flip_x):
        y = 1 - place.y if flip_y else place.y
        x = 1 - place.x if flip_x else place.x
        return place.at(place.shifted(d), y, x)

    def loader(ref, *index):
        return lambda start, size: ref[(*index, pl.ds(start, size), slice(None))]

    def put(dst, d, half, sums, stats):
        for c in range(combos):
            dst[d, half, c * per : (c + 1) * per, :] = sums[c].astype(BF16)
        dst[d, half, combos * per : (combos + 1) * per, :] = stats.astype(BF16)

    def hand_over(d, half):
        across = parts_ref.at[owner(d, 1, 1), half]
        if half == 0:
            go(0, d, half, across, from_diag, place.beside_x)
        else:
            go(0, d, half, across, from_diag, place.beside_y)

    def hand_beside(d, half):
        if half == 0:
            go(1, d, half, parts_ref.at[owner(d, 0, 1), half], from_x, place.beside_x)
        else:
            go(2, d, half, parts_ref.at[owner(d, 1, 0), half], from_y, place.beside_y)

    def pass_on(d, half):
        arrive(0, d, half, from_diag)
        mine = owner(d, 1, 0) if half == 0 else owner(d, 0, 1)
        pieces = (loader(parts_ref, mine, half), loader(from_diag, d, half))
        sums, stats, _ = merge(pieces, combos, per, scale)
        put(to_diag, d, half, sums, stats)
        if half == 0:
            go(2, d, half, to_diag.at[d, half], from_y, place.beside_y)
        else:
            go(1, d, half, to_diag.at[d, half], from_x, place.beside_x)

    def plane(d, half):
        arrive(1, d, half, from_x)
        arrive(2, d, half, from_y)
        pieces = (
            loader(parts_ref, owner(d, 0, 0), half),
            loader(from_x, d, half),
            loader(from_y, d, half),
        )
        sums, stats, _ = merge(pieces, combos, per, scale)
        put(to_line, d, half, sums, stats)
        if d:
            go(3, d, half, to_line.at[d, half], from_line, place.line(d))

    far = near[::-1] + [0]

    def hand_all(half):
        for d in far:
            hand_over(d, half)
            hand_beside(d, half)

    tokens = cands * toks

    def conclude(half):
        for d in range(1, depth):
            arrive(3, d, half, from_line)
        sums, _, denominator = merge(
            [loader(to_line, 0, half)] + [loader(from_line, d, half) for d in range(1, depth)],
            combos,
            per,
            scale,
        )
        denominator = pltpu.roll(denominator, 64, 1)
        for c in range(combos):
            at = (half * combos + c) * per
            ordered[at : at + per, :] = sums[c] / denominator[:, c : c + 1]
        for hh in range(pair):
            h = half * pair + hh
            block = [
                ordered[pl.ds(h * tokens * group + g, tokens, stride=group), :]
                for g in range(group)
            ]
            at = hh * tokens * group
            gathered[place.me, half, at : at + tokens * group, :] = jnp.concatenate(
                block, axis=0
            ).astype(BF16)

    tell = Gather(place, gathered, send, recv)

    def project(i, carry):
        steps = kv * group // 4
        start_row = pl.multiple_of((i % steps) * 2 * tokens, 2 * tokens)
        both = gathered[:, i // steps, pl.ds(start_row, 2 * tokens), :].astype(F32)
        left = both[:, :tokens, :].reshape(ranges * tokens, head).astype(BF16)
        right = both[:, tokens:, :].reshape(ranges * tokens, head).astype(BF16)
        rows_at = pl.multiple_of(i * 2 * head, 2 * head)
        total[...] += jnp.dot(
            jnp.concatenate([left, right], axis=1),
            weight[pl.ds(rows_at, 2 * head), :],
            preferred_element_type=F32,
        )
        return carry

    part = functools.partial
    nothing = lambda: None
    tiles = ranges // tile_owners

    def attend_all(half, first, second):
        for tile in range(tiles):
            last = tile == tiles - 1
            attend(half, tile, (first if last else nothing, second if last else nothing))

    ask.settle(0)
    attend_all(0, nothing, nothing)
    hand_all(0)
    ask.settle(1)
    early = depth // 2
    attend_all(
        1,
        lambda: run_all([part(pass_on, d, 0) for d in far[:early]]),
        lambda: run_all(
            [part(pass_on, d, 0) for d in far[early:]] + [part(plane, d, 0) for d in far[:early]]
        ),
    )
    hand_all(1)
    run_all([part(plane, d, 0) for d in far[early:]])
    conclude(0)
    tell.begin(0)
    reduce_one = [part(pass_on, d, 1) for d in far[:2]]
    for i, d in enumerate(far):
        if i + 2 < depth:
            reduce_one.append(part(pass_on, far[i + 2], 1))
        reduce_one.append(part(plane, d, 1))
    spread_zero = [part(tell.spread, d, 0) for d in near]
    relay_zero = [part(tell.relay, d, 0) for d in [0] + near]
    tell_zero = spread_zero[:2] + relay_zero[:1]
    for i in range(2, len(near)):
        tell_zero += [spread_zero[i], relay_zero[i - 1]]
    tell_zero += relay_zero[len(near) - 1 :]
    run_all(weave(reduce_one, tell_zero))
    conclude(1)
    tell.begin(1)
    total[...] = jnp.zeros_like(total)
    tell.settle(0)
    weight_fetch.wait()
    count_half = kv * group // 4
    lax.fori_loop(0, count_half, project, 0)
    for i, d in enumerate([0] + near):
        for other in near[:2] if i == 0 else near[i + 1 : i + 2]:
            tell.spread(other, 1)
        tell.relay(d, 1)
    tell.settle(1)
    lax.fori_loop(count_half, 2 * count_half, project, 0)
    half_rows = ranges * tokens // 2
    tp = lax.axis_index("tp")
    away[...] = total[
        pl.ds(pl.multiple_of((1 - tp) * half_rows, half_rows), half_rows), :
    ].astype(BF16)
    swap = pltpu.make_async_remote_copy(
        src_ref=away,
        dst_ref=arrived,
        send_sem=tp_sems.at[0],
        recv_sem=tp_sems.at[1],
        device_id={"tp": 1 - tp},
        device_id_type=MESH,
    )
    swap.start()
    ask.finish()
    tell.finish()
    for one in sent:
        one.wait_send()
    swap.wait()
    mine = total[pl.ds(pl.multiple_of(tp * half_rows, half_rows), half_rows), :]
    columns = total.shape[1]
    joined = mine + arrived[...].astype(F32)
    owners, size = ranges // 2, ranges // 2 * toks
    for c in range(columns // 128):
        lines[c, 0] = joined[:, c * 128 : (c + 1) * 128]
        for j in range(cands):
            for t in range(toks):
                lines[c, 1, pl.ds(j * size + t, owners, stride=toks), :] = lines[
                    c, 0, pl.ds(j * toks + t, owners, stride=tokens), :
                ]
            out_ref[j, :, c * 128 : (c + 1) * 128] = lines[
                c, 1, j * size : (j + 1) * size, :
            ].astype(BF16)


def on_device(
    queries,
    cand_keys,
    candidate_values,
    cached_prompt_keys,
    cached_prompt_values,
    block_lists,
    out_weight,
):
    cands, toks, heads, head = queries.shape
    kv = cand_keys.shape[2]
    group = heads // kv
    blocks, block_tokens = cached_prompt_keys.shape[:2]
    ranges = lax.axis_size("ctx")
    depth = ranges // 4
    piece = cands * toks * heads
    per = toks * group
    pair = kv // 2
    vmem = pl.BlockSpec(memory_space=pltpu.VMEM)
    anywhere = pl.BlockSpec(memory_space=pl.ANY)
    tile_owners = min(ranges, 256 // per)
    rows = tile_owners * per
    half_rows = piece // 2 + per
    most = min(blocks, cands * block_lists.shape[1] // ranges)
    entries = most + (cands - 1) * most // 2
    slots = ((entries + cands) // 2 + 1) // 2 * 2
    columns = out_weight.shape[1]
    tokens = cands * toks
    half = ranges * tokens // 2
    semaphores = [pltpu.SemaphoreType.DMA((4, depth, 2))] * 2
    block = pltpu.VMEM((depth, 2, half_rows, head), BF16)
    sizes = (cands, toks, kv, group, head, tile_owners, slots)
    cache = (blocks, block_tokens * kv, head)
    return pl.pallas_call(
        functools.partial(fused_kernel, ranges, sizes),
        out_shape=jax.ShapeDtypeStruct((cands, ranges * toks // 2, columns), BF16),
        in_specs=[pl.BlockSpec(memory_space=pltpu.SMEM)] + [vmem] * 4 + [anywhere] * 3,
        out_specs=vmem,
        scratch_shapes=[
            pltpu.VMEM((ranges, 2, cands, toks, heads // 2, head), BF16),
            pltpu.VMEM((2, *cache), BF16),
            pltpu.VMEM((block_tokens * kv, head), F32),
            pltpu.VMEM((2, kv, blocks, block_tokens, head), BF16),
            pltpu.SMEM((6, slots), jnp.int32),
            pltpu.VMEM((pair, cands, rows, head), BF16),
            pltpu.VMEM((2, kv, block_tokens, head), BF16),
            pltpu.VMEM((pair, slots, 2, rows, block_tokens), F32),
            pltpu.VMEM((pair, slots + 1, rows, block_tokens), F32),
            pltpu.VMEM((pair, slots + 1, rows, head), F32),
            pltpu.VMEM((pair, cands, rows, block_tokens), F32),
            pltpu.VMEM((pair, cands, rows, block_tokens), F32),
            pltpu.VMEM((pair, cands, rows, head), F32),
            pltpu.VMEM((ranges, 2, half_rows, head), BF16),
        ]
        + [block] * 6
        + [
            pltpu.VMEM((ranges, 2, piece // 2, head), BF16),
            pltpu.VMEM((piece, head), F32),
            pltpu.VMEM(out_weight.shape, BF16),
            pltpu.VMEM((2 * half, columns), F32),
            pltpu.VMEM((half, columns), BF16),
            pltpu.VMEM((half, columns), BF16),
            pltpu.VMEM((columns // 128, 2, half, 128), F32),
            pltpu.SemaphoreType.DMA((3,)),
            *semaphores,
            *semaphores,
            *semaphores,
            pltpu.SemaphoreType.DMA((2,)),
        ],
        compiler_params=pltpu.CompilerParams(
            collective_id=0, has_side_effects=True, vmem_limit_bytes=60 * 1024 * 1024
        ),
        name="verify",
    )(
        block_lists,
        block_lists,
        queries,
        cand_keys,
        candidate_values,
        cached_prompt_keys.reshape(cache),
        cached_prompt_values.reshape(cache),
        out_weight,
    )


def solution(mesh):
    placed = (
        P("groups", "ctx", "tp", None),
        P("groups", "ctx", "tp", None),
        P("groups", "ctx", "tp", None),
        P(("groups", "ctx"), None, "tp", None),
        P(("groups", "ctx"), None, "tp", None),
        P("groups", None),
        P("tp", "ctx"),
    )
    return jax.shard_map(
        on_device, mesh=mesh, in_specs=placed, out_specs=P("groups", "tp", "ctx"), check_vma=False
    )
```

```python
import functools
import math

import jax
import jax.numpy as jnp
from jax import lax
from jax.experimental import pallas as pl
from jax.experimental.pallas import tpu as pltpu
from jax.sharding import PartitionSpec as P

NEGATIVE = -1e30
MESH = pl.DeviceIdType.MESH
F32, BF16 = jnp.float32, jnp.bfloat16


class Place:
    def __init__(self, ranges):
        self.me = lax.axis_index("ctx")
        self.depth = ranges // 4
        self.x, self.y, self.z = self.me % 2, (self.me // 2) % 2, self.me // 4
        self.beside_x = self.at(self.z, self.y, 1 - self.x)
        self.beside_y = self.at(self.z, 1 - self.y, self.x)

    def at(self, z, y, x):
        return z * 4 + y * 2 + x

    def shifted(self, d):
        return (self.z + d + self.depth) % self.depth

    def line(self, d):
        return self.at(self.shifted(d), self.y, self.x)


def greet(place, with_tp):
    barrier = pltpu.get_barrier_semaphore()
    others = [place.line(d) for d in range(1, place.depth)]
    for other in others + [place.beside_x, place.beside_y]:
        pl.semaphore_signal(barrier, inc=1, device_id={"ctx": other}, device_id_type=MESH)
    if with_tp:
        pl.semaphore_signal(
            barrier, inc=1, device_id={"tp": 1 - lax.axis_index("tp")}, device_id_type=MESH
        )
    pl.semaphore_wait(barrier, place.depth + 1 + int(with_tp))


def near_first(depth):
    order = []
    for step in range(1, depth // 2 + 1):
        order += [step] + ([depth - step] if depth - step != step else [])
    return order


def merge(pieces, combos, per, scale):
    full = combos * per
    stats = [load(full, per).astype(F32) for load in pieces]
    peak = functools.reduce(jnp.maximum, stats)
    low = lax.broadcasted_iota(jnp.int32, (per, 128), 1) < 64
    scales = [jnp.exp2((jnp.where(low, s - peak, 0.0)) * scale) for s in stats]
    total = sum(pltpu.roll(w, 64, 1) * s for w, s in zip(scales, stats))
    sums = []
    for c in range(combos):
        sums.append(
            sum(
                load(c * per, per).astype(F32) * w[:, c : c + 1]
                for load, w in zip(pieces, scales)
            )
        )
    return sums, jnp.where(low, peak, total), total


class Gather:
    def __init__(self, place, buf, send, recv):
        self.place, self.buf, self.send, self.recv = place, buf, send, recv
        self.z_of = [place.shifted(-d) for d in range(place.depth)]

    def go(self, piece, slot, half, target):
        pltpu.make_async_remote_copy(
            src_ref=piece,
            dst_ref=piece,
            send_sem=self.send,
            recv_sem=self.recv.at[slot, half],
            device_id={"ctx": target},
            device_id_type=MESH,
        ).start()

    def wait(self, count, slot, half):
        some = self.buf.at[pl.ds(0, count), half]
        pltpu.make_async_copy(some, some, self.recv.at[slot, half]).wait()

    def begin(self, half):
        place = self.place
        self.spread(0, half)
        for d in near_first(place.depth)[::-1]:
            self.go(self.buf.at[place.me, half], d, half, place.line(d))

    def spread(self, d, half):
        place = self.place
        owner = place.at(self.z_of[d], place.y, place.x)
        if d:
            self.wait(1, d, half)
        for target in (place.beside_x, place.beside_y):
            self.go(self.buf.at[owner, half], place.depth + d, half, target)

    def relay(self, d, half):
        place = self.place
        self.wait(2, place.depth + d, half)
        size = self.buf.shape[2] // 2
        from_x = place.at(self.z_of[d], place.y, 1 - place.x)
        from_y = place.at(self.z_of[d], 1 - place.y, place.x)
        self.go(self.buf.at[from_x, half, pl.ds(0, size)], 0, half, place.beside_y)
        self.go(self.buf.at[from_y, half, pl.ds(size, size)], 0, half, place.beside_x)

    def settle(self, half):
        self.wait(self.place.depth, 0, half)

    def finish(self):
        away = self.buf.at[pl.ds(0, self.buf.shape[0] - 1)]
        pltpu.make_async_copy(away, away, self.send).wait()


def run_all(steps):
    for step in steps:
        step()


def fused_kernel(
    ranges,
    sizes,
    lists_smem,
    lists_ref,
    q_ref,
    own_k_ref,
    own_v_ref,
    k_ref,
    v_ref,
    weight_ref,
    out_ref,
    everyone,
    raw,
    wide,
    heads,
    plan,
    queries,
    own_blocks,
    scores,
    run,
    acc,
    peaks,
    own_sums,
    own_acc,
    parts_ref,
    from_diag,
    from_x,
    from_y,
    from_line,
    to_diag,
    to_line,
    gathered,
    ordered,
    weight,
    total,
    away,
    arrived,
    lines,
    in_sems,
    ask_send,
    ask_recv,
    red_send,
    red_recv,
    send,
    recv,
    tp_sems,
):
    cands, toks, kv, group, head, tile_owners, slots = sizes
    place = Place(ranges)
    depth = place.depth
    per = toks * group
    pair = kv // 2
    scale = head ** (-0.5) * math.log2(math.e)
    rows = tile_owners * per
    blocks, block_tokens = raw.shape[1], raw.shape[2] // kv
    sources = (k_ref, v_ref)
    fetches = [pltpu.make_async_copy(sources[n], raw.at[n], in_sems.at[n]) for n in range(2)]
    for fetch in fetches:
        fetch.start()
    weight_fetch = pltpu.make_async_copy(weight_ref, weight, in_sems.at[2])
    for half in range(2):
        everyone[place.me, half] = q_ref[:, :, half * pair * group : (half + 1) * pair * group, :]
    greet(place, True)

    ask = Gather(place, everyone, ask_send, ask_recv)
    near = near_first(depth)
    ask.begin(0)
    ask.begin(1)

    lowest = place.me * blocks
    listed = lists_smem.shape[1]
    below, count, start = [], [], [jnp.int32(0)]
    for j in range(cands):
        line = lists_ref[j : j + 1, :]
        below.append(jnp.sum((line < lowest).astype(jnp.int32)))
        count.append(jnp.sum((line < lowest + blocks).astype(jnp.int32)) - below[j])
        start.append(jnp.minimum(start[j] + (count[j] + 1) // 2, slots))

    def plan_slot(i, carry):
        cand, begun, under, many = jnp.int32(0), jnp.int32(0), below[0], count[0]
        for j in range(1, cands):
            here = i >= start[j]
            cand = jnp.where(here, j, cand)
            begun = jnp.where(here, start[j], begun)
            under = jnp.where(here, below[j], under)
            many = jnp.where(here, count[j], many)
        offset = 2 * (i - begun)
        plan[0, i] = cand
        for n in range(2):
            entry = jnp.minimum(under + offset + n, listed - 1)
            block = lists_smem[cand, entry] - lowest
            plan[1 + n, i] = jnp.minimum(jnp.maximum(block, 0), blocks - 1)
            plan[3 + n, i] = (offset + n < many).astype(jnp.int32)
        plan[5, i] = (offset == 0).astype(jnp.int32)
        return carry

    lax.fori_loop(0, slots, plan_slot, 0)

    def sort_heads(n, first, last):
        def one(b, carry):
            wide[...] = raw[n, b].astype(F32)
            for h in range(kv):
                heads[n, h, b] = wide[pl.ds(h, block_tokens, stride=kv), :].astype(BF16)
            return carry

        lax.fori_loop(first, last, one, 0)

    key_row = lax.broadcasted_iota(jnp.int32, (block_tokens, head), 0)

    def own_rows():
        for n, ref in enumerate((own_k_ref, own_v_ref)):
            mine = [ref[j].astype(F32) for j in range(cands)]
            for h in range(kv):
                block = jnp.zeros((block_tokens, head), F32)
                for j in range(cands):
                    for t in range(toks):
                        block = jnp.where(
                            key_row == j * toks + t, mine[j][t, h : h + 1, :], block
                        )
                own_blocks[n, h] = block.astype(BF16)

    def sort_step(n, part):
        def step():
            if part == 0:
                fetches[n].wait()
            sort_heads(n, part * (blocks // 4), (part + 1) * (blocks // 4))

        return step

    part = functools.partial

    def each(step, ds, half):
        return [part(step, d, half) for d in ds]

    come = near[::-1]
    run_all([sort_step(0, i) for i in range(4)])
    ask.relay(0, 0)
    run_all(each(ask.spread, come[:1], 0) + [sort_step(1, 0)])
    weight_fetch.start()
    run_all(each(ask.spread, come[1:], 0) + [sort_step(1, 1)])
    ask.relay(0, 1)
    run_all(each(ask.spread, come, 1) + [sort_step(1, 2), sort_step(1, 3), own_rows])
    run_all(each(ask.relay, come, 0))

    nt = (((1,), (1,)), ((), ()))
    row = lax.broadcasted_iota(jnp.int32, (rows, block_tokens), 0)
    lane = lax.broadcasted_iota(jnp.int32, (rows, block_tokens), 1)
    unroll = max(n for n in range(1, 12) if slots % n == 0)

    def attend(half, tile, between):
        owners = pl.ds(tile * tile_owners, tile_owners)
        query_pos = tile * tile_owners * toks + row // group

        def own_seen(j):
            t = lane - j * toks
            return (t >= 0) & (t < toks) & (place.me * toks + t <= query_pos)

        for hh in range(pair):
            run[hh, 0] = jnp.full((rows, block_tokens), NEGATIVE, F32)
            acc[hh, 0] = jnp.zeros((rows, head), F32)
            for j in range(cands):
                q = everyone[owners, half, j, :, hh * group : (hh + 1) * group, :].astype(F32)
                queries[hh, j] = q.reshape(rows, head).astype(BF16)

        def first_pass(it, carry):
            for u in range(unroll):
                i = it * unroll + u
                cand, fresh = plan[0, i], plan[5, i] > 0
                for hh in range(pair):
                    h = half * pair + hh
                    keys = jnp.concatenate(
                        [heads[0, h, plan[1, i]], heads[0, h, plan[2, i]]], axis=0
                    )
                    s = lax.dot_general(queries[hh, cand], keys, nt, preferred_element_type=F32)
                    top = jnp.where(fresh, NEGATIVE, run[hh, i])
                    for n in range(2):
                        one = s[:, n * block_tokens : (n + 1) * block_tokens]
                        one = jnp.where(plan[3 + n, i] > 0, one, NEGATIVE)
                        scores[hh, i, n] = one
                        top = jnp.maximum(top, one)
                    run[hh, i + 1] = top
            return carry

        lax.fori_loop(0, slots // unroll, first_pass, 0)
        between[0]()
        for hh in range(pair):
            h = half * pair + hh
            for j in range(cands):
                seen = own_seen(j)
                own = lax.dot_general(
                    queries[hh, j], own_blocks[0, h], nt, preferred_element_type=F32
                )
                own = jnp.where(seen, own, NEGATIVE)
                top = jnp.where(count[j] > 0, run[hh, start[j + 1]], NEGATIVE)
                top = jnp.maximum(top, own)
                peak = jnp.max(top, axis=1, keepdims=True).astype(BF16).astype(F32)
                p = jnp.where(seen, jnp.exp2((own - peak) * scale), 0.0)
                own_sums[hh, j] = p
                own_acc[hh, j] = jnp.dot(
                    p.astype(BF16), own_blocks[1, h], preferred_element_type=F32
                )
                peaks[hh, j] = jnp.broadcast_to(peak, (rows, block_tokens))
        between[1]()

        def second_pass(it, carry):
            for u in range(unroll):
                i = it * unroll + u
                cand, fresh = plan[0, i], plan[5, i] > 0
                for hh in range(pair):
                    h = half * pair + hh
                    peak = peaks[hh, cand]
                    p = [jnp.exp2((scores[hh, i, n] - peak) * scale) for n in range(2)]
                    run[hh, i + 1] = jnp.where(fresh, 0.0, run[hh, i]) + (p[0] + p[1])
                    values = jnp.concatenate(
                        [heads[1, h, plan[1, i]], heads[1, h, plan[2, i]]], axis=0
                    )
                    weights = jnp.concatenate([one.astype(BF16) for one in p], axis=1)
                    acc[hh, i + 1] = jnp.where(fresh, 0.0, acc[hh, i]) + jnp.dot(
                        weights, values, preferred_element_type=F32
                    )
            return carry

        middle = slots // unroll // 2
        lax.fori_loop(0, middle, second_pass, 0)
        between[2]()
        lax.fori_loop(middle, slots // unroll, second_pass, 0)
        between[3]()
        lanes = lax.broadcasted_iota(jnp.int32, (rows, 128), 1)
        for hh in range(pair):
            stats = jnp.zeros((rows, 128), F32)
            for j in range(cands):
                last, some = start[j + 1], count[j] > 0
                sums = jnp.where(some, run[hh, last], 0.0) + own_sums[hh, j]
                found = jnp.where(some, acc[hh, last], 0.0) + own_acc[hh, j]
                stats = jnp.where(lanes == j, peaks[hh, j], stats)
                stats = jnp.where(
                    lanes == 64 + j, jnp.sum(sums, axis=1, keepdims=True), stats
                )
                parts_ref[owners, half, hh, j * per : (j + 1) * per, :] = found.reshape(
                    tile_owners, per, head
                ).astype(BF16)
            parts_ref[owners, half, hh, cands * per : (cands + 1) * per, :] = stats.reshape(
                tile_owners, per, 128
            ).astype(BF16)

    def go(slot, half, src, dst, target):
        pltpu.make_async_remote_copy(
            src_ref=src,
            dst_ref=dst,
            send_sem=red_send,
            recv_sem=red_recv.at[slot, half],
            device_id={"ctx": target},
            device_id_type=MESH,
        ).start()

    def arrive(slot, half, some):
        pltpu.make_async_copy(some, some, red_recv.at[slot, half]).wait()

    def owner(d, flip_y, flip_x):
        y = 1 - place.y if flip_y else place.y
        x = 1 - place.x if flip_x else place.x
        return place.at(place.shifted(d), y, x)

    def loader(ref, *index):
        return lambda start, size: ref[(*index, pl.ds(start, size), slice(None))]

    def put(dst, index, sums, stats):
        for c in range(cands):
            dst[(*index, slice(c * per, (c + 1) * per), slice(None))] = sums[c].astype(BF16)
        dst[(*index, slice(cands * per, (cands + 1) * per), slice(None))] = stats.astype(BF16)

    def hand_over(d, half):
        across = owner(d, 1, 1)
        for u, target in enumerate((place.beside_x, place.beside_y)):
            go(d, half, parts_ref.at[across, half, u], from_diag.at[d, half, u], target)

    def hand_beside(d, half):
        x_owner, y_owner = owner(d, 0, 1), owner(d, 1, 0)
        slot = depth + d
        go(slot, half, parts_ref.at[x_owner, half, 0], from_x.at[d, half, 0], place.beside_x)
        go(slot, half, parts_ref.at[y_owner, half, 1], from_y.at[d, half, 1], place.beside_y)

    def pass_on(d, half):
        arrive(d, half, from_diag.at[d, half])
        for u in range(2):
            mine = owner(d, 1, 0) if u == 0 else owner(d, 0, 1)
            pieces = (loader(parts_ref, mine, half, u), loader(from_diag, d, half, u))
            sums, stats, _ = merge(pieces, cands, per, scale)
            put(to_diag, (d, half, u), sums, stats)
            into, target = (from_y, place.beside_y) if u == 0 else (from_x, place.beside_x)
            go(depth + d, half, to_diag.at[d, half, u], into.at[d, half, u], target)

    def plane(d, half):
        arrive(depth + d, half, parts_ref.at[pl.ds(0, 2), half])
        for u in range(2):
            pieces = (
                loader(parts_ref, owner(d, 0, 0), half, u),
                loader(from_x, d, half, u),
                loader(from_y, d, half, u),
            )
            sums, stats, _ = merge(pieces, cands, per, scale)
            put(to_line, (d, half, u), sums, stats)
        if d:
            go(2 * depth, half, to_line.at[d, half], from_line.at[d, half], place.line(d))

    far = near[::-1] + [0]

    def hand_all(half):
        for d in far:
            hand_over(d, half)
        for d in far:
            hand_beside(d, half)

    tokens = cands * toks

    def conclude(half):
        arrive(2 * depth, half, from_line.at[pl.ds(0, depth - 1), half])
        for u in range(2):
            lines_in = [loader(from_line, d, half, u) for d in range(1, depth)]
            sums, _, denominator = merge(
                [loader(to_line, 0, half, u)] + lines_in, cands, per, scale
            )
            inverse = 1.0 / pltpu.roll(denominator, 64, 1)
            for c in range(cands):
                at = ((half * 2 + u) * cands + c) * per
                ordered[at : at + per, :] = sums[c] * inverse[:, c : c + 1]
        for hh in range(pair):
            h = half * pair + hh
            block = [
                ordered[pl.ds(h * tokens * group + g, tokens, stride=group), :]
                for g in range(group)
            ]
            at = hh * tokens * group
            gathered[place.me, half, at : at + tokens * group, :] = jnp.concatenate(
                block, axis=0
            ).astype(BF16)

    tell = Gather(place, gathered, send, recv)

    def project(i, carry):
        steps = kv * group // 4
        start_row = pl.multiple_of((i % steps) * 2 * tokens, 2 * tokens)
        both = gathered[:, i // steps, pl.ds(start_row, 2 * tokens), :].astype(F32)
        left = both[:, :tokens, :].reshape(ranges * tokens, head).astype(BF16)
        right = both[:, tokens:, :].reshape(ranges * tokens, head).astype(BF16)
        rows_at = pl.multiple_of(i * 2 * head, 2 * head)
        total[...] += jnp.dot(
            jnp.concatenate([left, right], axis=1),
            weight[pl.ds(rows_at, 2 * head), :],
            preferred_element_type=F32,
        )
        return carry

    tiles = ranges // tile_owners

    def attend_all(half, *steps):
        for tile in range(tiles):
            last = tile == tiles - 1
            attend(half, tile, [part(run_all, some if last else []) for some in steps])

    ask.settle(0)
    attend_all(0, each(ask.relay, come, 1), [], [], [])
    hand_all(0)
    ask.settle(1)
    early = depth // 2
    attend_all(
        1,
        each(pass_on, far[:early], 0),
        each(pass_on, far[early:], 0),
        each(plane, far[:early], 0),
        each(plane, far[early:], 0),
    )
    hand_all(1)
    run_all(each(pass_on, far[:early], 1))
    conclude(0)
    tell.begin(0)
    run_all(each(pass_on, far[early:], 1))
    run_all(each(plane, far, 1))
    run_all(each(tell.relay, [0], 0) + each(tell.spread, come, 0))
    conclude(1)
    tell.begin(1)
    total[...] = jnp.zeros_like(total)
    weight_fetch.wait()
    run_all(each(tell.relay, come, 0))
    count_half = kv * group // 4
    tell.settle(0)

    def project_some(index, of):
        lax.fori_loop(index * count_half // of, (index + 1) * count_half // of, project, 0)

    run_all(each(tell.relay, [0], 1) + each(tell.spread, come[:-1], 1))
    project_some(0, 2)
    run_all(each(tell.spread, come[-1:], 1))
    project_some(1, 2)
    run_all(each(tell.relay, come, 1))
    tell.settle(1)
    lax.fori_loop(count_half, 2 * count_half, project, 0)
    half_rows = ranges * tokens // 2
    tp = lax.axis_index("tp")
    away[...] = total[
        pl.ds(pl.multiple_of((1 - tp) * half_rows, half_rows), half_rows), :
    ].astype(BF16)
    swap = pltpu.make_async_remote_copy(
        src_ref=away,
        dst_ref=arrived,
        send_sem=tp_sems.at[0],
        recv_sem=tp_sems.at[1],
        device_id={"tp": 1 - tp},
        device_id_type=MESH,
    )
    swap.start()
    ask.finish()
    tell.finish()
    handed = parts_ref.at[pl.ds(0, ranges - 1)]
    pltpu.make_async_copy(handed, handed, red_send).wait()
    swap.wait()
    mine = total[pl.ds(pl.multiple_of(tp * half_rows, half_rows), half_rows), :]
    columns = total.shape[1]
    joined = mine + arrived[...].astype(F32)
    owners, size = ranges // 2, ranges // 2 * toks
    for c in range(columns // 128):
        lines[c, 0] = joined[:, c * 128 : (c + 1) * 128]
        for j in range(cands):
            for t in range(toks):
                lines[c, 1, pl.ds(j * size + t, owners, stride=toks), :] = lines[
                    c, 0, pl.ds(j * toks + t, owners, stride=tokens), :
                ]
            out_ref[j, :, c * 128 : (c + 1) * 128] = lines[
                c, 1, j * size : (j + 1) * size, :
            ].astype(BF16)


def on_device(
    queries,
    cand_keys,
    candidate_values,
    cached_prompt_keys,
    cached_prompt_values,
    block_lists,
    out_weight,
):
    cands, toks, heads, head = queries.shape
    kv = cand_keys.shape[2]
    group = heads // kv
    blocks, block_tokens = cached_prompt_keys.shape[:2]
    ranges = lax.axis_size("ctx")
    depth = ranges // 4
    piece = cands * toks * heads
    per = toks * group
    pair = kv // 2
    vmem = pl.BlockSpec(memory_space=pltpu.VMEM)
    anywhere = pl.BlockSpec(memory_space=pl.ANY)
    tile_owners = min(ranges, 256 // per)
    rows = tile_owners * per
    unit_rows = cands * per + per
    most = min(blocks, cands * block_lists.shape[1] // ranges)
    entries = most + (cands - 1) * most // 2
    slots = ((entries + cands) // 2 + 1) // 2 * 2
    columns = out_weight.shape[1]
    tokens = cands * toks
    half = ranges * tokens // 2
    dma = pltpu.SemaphoreType.DMA
    semaphores = lambda slots: [dma, dma((slots, 2))]
    block = pltpu.VMEM((depth, 2, pair, unit_rows, head), BF16)
    sizes = (cands, toks, kv, group, head, tile_owners, slots)
    cache = (blocks, block_tokens * kv, head)
    return pl.pallas_call(
        functools.partial(fused_kernel, ranges, sizes),
        out_shape=jax.ShapeDtypeStruct((cands, ranges * toks // 2, columns), BF16),
        in_specs=[pl.BlockSpec(memory_space=pltpu.SMEM)] + [vmem] * 4 + [anywhere] * 3,
        out_specs=vmem,
        scratch_shapes=[
            pltpu.VMEM((ranges, 2, cands, toks, heads // 2, head), BF16),
            pltpu.VMEM((2, *cache), BF16),
            pltpu.VMEM((block_tokens * kv, head), F32),
            pltpu.VMEM((2, kv, blocks, block_tokens, head), BF16),
            pltpu.SMEM((6, slots), jnp.int32),
            pltpu.VMEM((pair, cands, rows, head), BF16),
            pltpu.VMEM((2, kv, block_tokens, head), BF16),
            pltpu.VMEM((pair, slots, 2, rows, block_tokens), F32),
            pltpu.VMEM((pair, slots + 1, rows, block_tokens), F32),
            pltpu.VMEM((pair, slots + 1, rows, head), F32),
            pltpu.VMEM((pair, cands, rows, block_tokens), F32),
            pltpu.VMEM((pair, cands, rows, block_tokens), F32),
            pltpu.VMEM((pair, cands, rows, head), F32),
            pltpu.VMEM((ranges, 2, pair, unit_rows, head), BF16),
        ]
        + [block] * 6
        + [
            pltpu.VMEM((ranges, 2, piece // 2, head), BF16),
            pltpu.VMEM((piece, head), F32),
            pltpu.VMEM(out_weight.shape, BF16),
            pltpu.VMEM((2 * half, columns), F32),
            pltpu.VMEM((half, columns), BF16),
            pltpu.VMEM((half, columns), BF16),
            pltpu.VMEM((columns // 128, 2, half, 128), F32),
            pltpu.SemaphoreType.DMA((3,)),
            *semaphores(2 * depth),
            *semaphores(2 * depth + 1),
            *semaphores(2 * depth),
            pltpu.SemaphoreType.DMA((2,)),
        ],
        compiler_params=pltpu.CompilerParams(
            collective_id=0, has_side_effects=True, vmem_limit_bytes=60 * 1024 * 1024
        ),
        name="verify",
    )(
        block_lists,
        block_lists,
        queries,
        cand_keys,
        candidate_values,
        cached_prompt_keys.reshape(cache),
        cached_prompt_values.reshape(cache),
        out_weight,
    )


def solution(mesh):
    placed = (
        P("groups", "ctx", "tp", None),
        P("groups", "ctx", "tp", None),
        P("groups", "ctx", "tp", None),
        P(("groups", "ctx"), None, "tp", None),
        P(("groups", "ctx"), None, "tp", None),
        P("groups", None),
        P("tp", "ctx"),
    )
    return jax.shard_map(
        on_device, mesh=mesh, in_specs=placed, out_specs=P("groups", "tp", "ctx"), check_vma=False
    )
```

```python
import functools
import math

import jax
import jax.numpy as jnp
from jax import lax
from jax.experimental import pallas as pl
from jax.experimental.pallas import tpu as pltpu
from jax.sharding import PartitionSpec as P

NEGATIVE = -1e30
MESH = pl.DeviceIdType.MESH
F32, BF16 = jnp.float32, jnp.bfloat16


class Place:
    def __init__(self, ranges):
        self.me = lax.axis_index("ctx")
        self.depth = ranges // 4
        self.x, self.y, self.z = self.me % 2, (self.me // 2) % 2, self.me // 4
        self.beside_x = self.at(self.z, self.y, 1 - self.x)
        self.beside_y = self.at(self.z, 1 - self.y, self.x)

    def at(self, z, y, x):
        return z * 4 + y * 2 + x

    def shifted(self, d):
        return (self.z + d + self.depth) % self.depth

    def line(self, d):
        return self.at(self.shifted(d), self.y, self.x)


def greet(place):
    barrier = pltpu.get_barrier_semaphore()
    others = [place.line(d) for d in range(1, place.depth)]
    for other in others + [place.beside_x, place.beside_y]:
        pl.semaphore_signal(barrier, inc=1, device_id={"ctx": other}, device_id_type=MESH)
    pl.semaphore_signal(
        barrier, inc=1, device_id={"tp": 1 - lax.axis_index("tp")}, device_id_type=MESH
    )


def near_first(depth):
    order = []
    for step in range(1, depth // 2 + 1):
        order += [step] + ([depth - step] if depth - step != step else [])
    return order


def merge(pieces, combos, per, scale):
    full = combos * per
    stats = [load(full, per).astype(F32) for load in pieces]
    peak = functools.reduce(jnp.maximum, stats)
    low = lax.broadcasted_iota(jnp.int32, (per, 128), 1) < 64
    scales = [jnp.exp2((jnp.where(low, s - peak, 0.0)) * scale) for s in stats]
    total = sum(pltpu.roll(w, 64, 1) * s for w, s in zip(scales, stats))
    sums = []
    for c in range(combos):
        sums.append(
            sum(
                load(c * per, per).astype(F32) * w[:, c : c + 1]
                for load, w in zip(pieces, scales)
            )
        )
    return sums, jnp.where(low, peak, total), total


class Gather:
    def __init__(self, place, buf, send, recv):
        self.place, self.buf, self.send, self.recv = place, buf, send, recv
        self.z_of = [place.shifted(-d) for d in range(place.depth)]

    def go(self, piece, slot, half, target):
        pltpu.make_async_remote_copy(
            src_ref=piece,
            dst_ref=piece,
            send_sem=self.send,
            recv_sem=self.recv.at[slot, half],
            device_id={"ctx": target},
            device_id_type=MESH,
        ).start()

    def wait(self, count, slot, half):
        some = self.buf.at[pl.ds(0, count), half]
        pltpu.make_async_copy(some, some, self.recv.at[slot, half]).wait()

    def begin(self, half):
        place = self.place
        self.spread(0, half)
        for d in near_first(place.depth):
            self.go(self.buf.at[place.me, half], d, half, place.line(d))

    def spread(self, d, half):
        place = self.place
        owner = place.at(self.z_of[d], place.y, place.x)
        if d:
            self.wait(1, d, half)
        for target in (place.beside_x, place.beside_y):
            self.go(self.buf.at[owner, half], place.depth + d, half, target)

    def relay(self, d, half):
        place = self.place
        self.wait(2, place.depth + d, half)
        size = self.buf.shape[2] // 2
        from_x = place.at(self.z_of[d], place.y, 1 - place.x)
        from_y = place.at(self.z_of[d], 1 - place.y, place.x)
        self.go(self.buf.at[from_x, half, pl.ds(0, size)], 0, half, place.beside_y)
        self.go(self.buf.at[from_y, half, pl.ds(size, size)], 0, half, place.beside_x)

    def settle(self, half):
        self.wait(self.place.depth, 0, half)

    def finish(self):
        away = self.buf.at[pl.ds(0, self.buf.shape[0] - 1)]
        pltpu.make_async_copy(away, away, self.send).wait()


def run_all(steps):
    for step in steps:
        step()


def fused_kernel(
    ranges,
    sizes,
    lists_smem,
    lists_hbm,
    q_ref,
    own_k_hbm,
    own_v_hbm,
    k_ref,
    v_ref,
    weight_ref,
    out_ref,
    lists_ref,
    own_k_ref,
    own_v_ref,
    everyone,
    raw,
    wide,
    heads,
    plan,
    queries,
    own_blocks,
    scores,
    run,
    acc,
    peaks,
    own_sums,
    own_acc,
    parts_ref,
    from_diag,
    from_x,
    from_y,
    from_line,
    to_diag,
    to_line,
    gathered,
    ordered,
    weight,
    total,
    away,
    arrived,
    lines,
    in_sems,
    ask_send,
    ask_recv,
    red_send,
    red_recv,
    send,
    recv,
    tp_sems,
):
    cands, toks, kv, group, head, tile_owners, slots = sizes
    place = Place(ranges)
    depth = place.depth
    per = toks * group
    pair = kv // 2
    scale = head ** (-0.5) * math.log2(math.e)
    rows = tile_owners * per
    blocks, block_tokens = raw.shape[1], raw.shape[2] // kv
    greet(place)
    mine = [
        pltpu.make_async_copy(
            q_ref.at[:, :, pl.ds(half * pair * group, pair * group), :],
            everyone.at[place.me, half],
            in_sems.at[3],
        )
        for half in range(2)
    ]
    small = [(lists_hbm, lists_ref), (own_k_hbm, own_k_ref), (own_v_hbm, own_v_ref)]
    local = [
        pltpu.make_async_copy(src, dst, in_sems.at[4 + n]) for n, (src, dst) in enumerate(small)
    ]
    for one in mine + local:
        one.start()
    sources = (k_ref, v_ref)
    fetches = [pltpu.make_async_copy(sources[n], raw.at[n], in_sems.at[n]) for n in range(2)]
    for fetch in fetches:
        fetch.start()
    weight_fetch = pltpu.make_async_copy(weight_ref, weight, in_sems.at[2])
    whole = everyone.at[place.me]
    pltpu.make_async_copy(whole, whole, in_sems.at[3]).wait()
    pl.semaphore_wait(pltpu.get_barrier_semaphore(), depth + 2)

    ask = Gather(place, everyone, ask_send, ask_recv)
    near = near_first(depth)
    ask.begin(0)
    ask.begin(1)
    for one in local:
        one.wait()

    lowest = place.me * blocks
    listed = lists_smem.shape[1]
    below, count, start = [], [], [jnp.int32(0)]
    for j in range(cands):
        line = lists_ref[j : j + 1, :]
        below.append(jnp.sum((line < lowest).astype(jnp.int32)))
        count.append(jnp.sum((line < lowest + blocks).astype(jnp.int32)) - below[j])
        start.append(jnp.minimum(start[j] + (count[j] + 1) // 2, slots))

    def plan_slot(i, carry):
        cand, begun, under, many = jnp.int32(0), jnp.int32(0), below[0], count[0]
        for j in range(1, cands):
            here = i >= start[j]
            cand = jnp.where(here, j, cand)
            begun = jnp.where(here, start[j], begun)
            under = jnp.where(here, below[j], under)
            many = jnp.where(here, count[j], many)
        offset = 2 * (i - begun)
        plan[0, i] = cand
        for n in range(2):
            entry = jnp.minimum(under + offset + n, listed - 1)
            block = lists_smem[cand, entry] - lowest
            plan[1 + n, i] = jnp.minimum(jnp.maximum(block, 0), blocks - 1)
            plan[3 + n, i] = (offset + n < many).astype(jnp.int32)
        plan[5, i] = (offset == 0).astype(jnp.int32)
        return carry

    lax.fori_loop(0, slots, plan_slot, 0)

    def sort_heads(n, first, last):
        def one(b, carry):
            wide[...] = raw[n, b].astype(F32)
            for h in range(kv):
                heads[n, h, b] = wide[pl.ds(h, block_tokens, stride=kv), :].astype(BF16)
            return carry

        lax.fori_loop(first, last, one, 0)

    key_row = lax.broadcasted_iota(jnp.int32, (block_tokens, head), 0)

    def own_rows():
        for n, ref in enumerate((own_k_ref, own_v_ref)):
            mine = [ref[j].astype(F32) for j in range(cands)]
            for h in range(kv):
                block = jnp.zeros((block_tokens, head), F32)
                for j in range(cands):
                    for t in range(toks):
                        block = jnp.where(
                            key_row == j * toks + t, mine[j][t, h : h + 1, :], block
                        )
                own_blocks[n, h] = block.astype(BF16)

    def sort_step(n, part):
        def step():
            if part == 0:
                fetches[n].wait()
            sort_heads(n, part * (blocks // 4), (part + 1) * (blocks // 4))

        return step

    part = functools.partial

    def each(step, ds, half):
        return [part(step, d, half) for d in ds]

    come = near
    run_all([sort_step(0, i) for i in range(4)])
    ask.relay(0, 0)
    run_all(each(ask.spread, come[:1], 0) + [sort_step(1, 0)])
    weight_fetch.start()
    run_all(each(ask.spread, come[1:], 0) + [sort_step(1, 1)])
    ask.relay(0, 1)
    run_all(each(ask.spread, come, 1) + [sort_step(1, 2), sort_step(1, 3), own_rows])
    run_all(each(ask.relay, come, 0))

    nt = (((1,), (1,)), ((), ()))
    row = lax.broadcasted_iota(jnp.int32, (rows, block_tokens), 0)
    lane = lax.broadcasted_iota(jnp.int32, (rows, block_tokens), 1)
    unroll = max(n for n in range(1, 12) if slots % n == 0)

    def attend(half, tile, between):
        owners = pl.ds(tile * tile_owners, tile_owners)
        query_pos = tile * tile_owners * toks + row // group

        def own_seen(j):
            t = lane - j * toks
            return (t >= 0) & (t < toks) & (place.me * toks + t <= query_pos)

        for hh in range(pair):
            run[hh, 0] = jnp.full((rows, block_tokens), NEGATIVE, F32)
            acc[hh, 0] = jnp.zeros((rows, head), F32)
            for j in range(cands):
                q = everyone[owners, half, j, :, hh * group : (hh + 1) * group, :].astype(F32)
                queries[hh, j] = q.reshape(rows, head).astype(BF16)

        def first_pass(it, carry):
            for u in range(unroll):
                i = it * unroll + u
                cand, fresh = plan[0, i], plan[5, i] > 0
                for hh in range(pair):
                    h = half * pair + hh
                    keys = jnp.concatenate(
                        [heads[0, h, plan[1, i]], heads[0, h, plan[2, i]]], axis=0
                    )
                    s = lax.dot_general(queries[hh, cand], keys, nt, preferred_element_type=F32)
                    top = jnp.where(fresh, NEGATIVE, run[hh, i])
                    for n in range(2):
                        one = s[:, n * block_tokens : (n + 1) * block_tokens]
                        one = jnp.where(plan[3 + n, i] > 0, one, NEGATIVE)
                        scores[hh, i, n] = one
                        top = jnp.maximum(top, one)
                    run[hh, i + 1] = top
            return carry

        lax.fori_loop(0, slots // unroll, first_pass, 0)
        between[0]()
        for hh in range(pair):
            h = half * pair + hh
            for j in range(cands):
                seen = own_seen(j)
                own = lax.dot_general(
                    queries[hh, j], own_blocks[0, h], nt, preferred_element_type=F32
                )
                own = jnp.where(seen, own, NEGATIVE)
                top = jnp.where(count[j] > 0, run[hh, start[j + 1]], NEGATIVE)
                top = jnp.maximum(top, own)
                peak = jnp.max(top, axis=1, keepdims=True).astype(BF16).astype(F32)
                p = jnp.where(seen, jnp.exp2((own - peak) * scale), 0.0)
                own_sums[hh, j] = p
                own_acc[hh, j] = jnp.dot(
                    p.astype(BF16), own_blocks[1, h], preferred_element_type=F32
                )
                peaks[hh, j] = jnp.broadcast_to(peak, (rows, block_tokens))
        between[1]()

        def second_pass(it, carry):
            for u in range(unroll):
                i = it * unroll + u
                cand, fresh = plan[0, i], plan[5, i] > 0
                for hh in range(pair):
                    h = half * pair + hh
                    peak = peaks[hh, cand]
                    p = [jnp.exp2((scores[hh, i, n] - peak) * scale) for n in range(2)]
                    run[hh, i + 1] = jnp.where(fresh, 0.0, run[hh, i]) + (p[0] + p[1])
                    values = jnp.concatenate(
                        [heads[1, h, plan[1, i]], heads[1, h, plan[2, i]]], axis=0
                    )
                    weights = jnp.concatenate([one.astype(BF16) for one in p], axis=1)
                    acc[hh, i + 1] = jnp.where(fresh, 0.0, acc[hh, i]) + jnp.dot(
                        weights, values, preferred_element_type=F32
                    )
            return carry

        middle = slots // unroll // 2
        lax.fori_loop(0, middle, second_pass, 0)
        between[2]()
        lax.fori_loop(middle, slots // unroll, second_pass, 0)
        between[3]()
        lanes = lax.broadcasted_iota(jnp.int32, (rows, 128), 1)
        for hh in range(pair):
            stats = jnp.zeros((rows, 128), F32)
            for j in range(cands):
                last, some = start[j + 1], count[j] > 0
                sums = jnp.where(some, run[hh, last], 0.0) + own_sums[hh, j]
                found = jnp.where(some, acc[hh, last], 0.0) + own_acc[hh, j]
                stats = jnp.where(lanes == j, peaks[hh, j], stats)
                stats = jnp.where(
                    lanes == 64 + j, jnp.sum(sums, axis=1, keepdims=True), stats
                )
                parts_ref[owners, half, hh, j * per : (j + 1) * per, :] = found.reshape(
                    tile_owners, per, head
                ).astype(BF16)
            parts_ref[owners, half, hh, cands * per : (cands + 1) * per, :] = stats.reshape(
                tile_owners, per, 128
            ).astype(BF16)

    def go(slot, half, src, dst, target):
        pltpu.make_async_remote_copy(
            src_ref=src,
            dst_ref=dst,
            send_sem=red_send,
            recv_sem=red_recv.at[slot, half],
            device_id={"ctx": target},
            device_id_type=MESH,
        ).start()

    def arrive(slot, half, some):
        pltpu.make_async_copy(some, some, red_recv.at[slot, half]).wait()

    def owner(d, flip_y, flip_x):
        y = 1 - place.y if flip_y else place.y
        x = 1 - place.x if flip_x else place.x
        return place.at(place.shifted(d), y, x)

    def loader(ref, *index):
        return lambda start, size: ref[(*index, pl.ds(start, size), slice(None))]

    def put(dst, index, sums, stats):
        for c in range(cands):
            dst[(*index, slice(c * per, (c + 1) * per), slice(None))] = sums[c].astype(BF16)
        dst[(*index, slice(cands * per, (cands + 1) * per), slice(None))] = stats.astype(BF16)

    def hand_over(d, half):
        across = owner(d, 1, 1)
        for u, target in enumerate((place.beside_x, place.beside_y)):
            go(d, half, parts_ref.at[across, half, u], from_diag.at[d, half, u], target)

    def hand_beside(d, half):
        x_owner, y_owner = owner(d, 0, 1), owner(d, 1, 0)
        slot = depth + d
        go(slot, half, parts_ref.at[x_owner, half, 0], from_x.at[d, half, 0], place.beside_x)
        go(slot, half, parts_ref.at[y_owner, half, 1], from_y.at[d, half, 1], place.beside_y)

    def pass_on(d, half):
        arrive(d, half, from_diag.at[d, half])
        for u in range(2):
            mine = owner(d, 1, 0) if u == 0 else owner(d, 0, 1)
            pieces = (loader(parts_ref, mine, half, u), loader(from_diag, d, half, u))
            sums, stats, _ = merge(pieces, cands, per, scale)
            put(to_diag, (d, half, u), sums, stats)
            into, target = (from_y, place.beside_y) if u == 0 else (from_x, place.beside_x)
            go(depth + d, half, to_diag.at[d, half, u], into.at[d, half, u], target)

    def plane(d, half):
        arrive(depth + d, half, parts_ref.at[pl.ds(0, 2), half])
        for u in range(2):
            pieces = (
                loader(parts_ref, owner(d, 0, 0), half, u),
                loader(from_x, d, half, u),
                loader(from_y, d, half, u),
            )
            sums, stats, _ = merge(pieces, cands, per, scale)
            put(to_line, (d, half, u), sums, stats)
        if d:
            go(2 * depth, half, to_line.at[d, half], from_line.at[d, half], place.line(d))

    far = near[::-1] + [0]

    def hand_all(half):
        for d in far:
            hand_over(d, half)
        for d in far:
            hand_beside(d, half)

    tokens = cands * toks

    def conclude(half):
        arrive(2 * depth, half, from_line.at[pl.ds(0, depth - 1), half])
        for u in range(2):
            lines_in = [loader(from_line, d, half, u) for d in range(1, depth)]
            sums, _, denominator = merge(
                [loader(to_line, 0, half, u)] + lines_in, cands, per, scale
            )
            inverse = 1.0 / pltpu.roll(denominator, 64, 1)
            for c in range(cands):
                at = ((half * 2 + u) * cands + c) * per
                ordered[at : at + per, :] = sums[c] * inverse[:, c : c + 1]
        for hh in range(pair):
            h = half * pair + hh
            block = [
                ordered[pl.ds(h * tokens * group + g, tokens, stride=group), :]
                for g in range(group)
            ]
            at = hh * tokens * group
            gathered[place.me, half, at : at + tokens * group, :] = jnp.concatenate(
                block, axis=0
            ).astype(BF16)

    tell = Gather(place, gathered, send, recv)

    count_half = kv * group // 2
    deep = math.gcd(count_half, 8)

    def project(i, carry):
        at = pl.multiple_of((i * deep) % count_half * tokens, deep * tokens)
        some = gathered[:, i * deep // count_half, pl.ds(at, deep * tokens), :].astype(F32)
        inputs = [
            some[:, n * tokens : (n + 1) * tokens, :].reshape(ranges * tokens, head).astype(BF16)
            for n in range(deep)
        ]
        total[...] += jnp.dot(
            jnp.concatenate(inputs, axis=1),
            weight[pl.ds(pl.multiple_of(i * deep * head, deep * head), deep * head), :],
            preferred_element_type=F32,
        )
        return carry

    tiles = ranges // tile_owners

    def attend_all(half, *steps):
        for tile in range(tiles):
            last = tile == tiles - 1
            attend(half, tile, [part(run_all, some if last else []) for some in steps])

    ask.settle(0)
    attend_all(0, each(ask.relay, come, 1), [], [], [])
    hand_all(0)
    ask.settle(1)
    early = depth // 2
    attend_all(
        1,
        each(pass_on, far[:early], 0),
        each(pass_on, far[early:], 0),
        [],
        each(plane, far, 0),
    )
    hand_all(1)
    run_all(each(pass_on, far, 1))
    conclude(0)
    run_all(each(plane, far, 1))
    tell.begin(0)
    conclude(1)
    tell.begin(1)
    total[...] = jnp.zeros_like(total)
    weight_fetch.wait()
    run_all(each(tell.relay, [0], 0) + each(tell.spread, come, 0))
    run_all(each(tell.relay, [0], 1) + each(tell.spread, come, 1))
    run_all(each(tell.relay, come, 0) + each(tell.relay, come, 1))
    steps = count_half // deep
    tell.settle(0)
    lax.fori_loop(0, steps, project, 0)
    tell.settle(1)
    lax.fori_loop(steps, 2 * steps, project, 0)
    half_rows = ranges * tokens // 2
    tp = lax.axis_index("tp")
    away[...] = total[
        pl.ds(pl.multiple_of((1 - tp) * half_rows, half_rows), half_rows), :
    ].astype(BF16)
    swap = pltpu.make_async_remote_copy(
        src_ref=away,
        dst_ref=arrived,
        send_sem=tp_sems.at[0],
        recv_sem=tp_sems.at[1],
        device_id={"tp": 1 - tp},
        device_id_type=MESH,
    )
    swap.start()
    ask.finish()
    tell.finish()
    handed = parts_ref.at[pl.ds(0, ranges - 1)]
    pltpu.make_async_copy(handed, handed, red_send).wait()
    swap.wait()
    mine = total[pl.ds(pl.multiple_of(tp * half_rows, half_rows), half_rows), :]
    columns = total.shape[1]
    joined = mine + arrived[...].astype(F32)
    owners, size = ranges // 2, ranges // 2 * toks
    for c in range(columns // 128):
        lines[c, 0] = joined[:, c * 128 : (c + 1) * 128]
        for j in range(cands):
            for t in range(toks):
                lines[c, 1, pl.ds(j * size + t, owners, stride=toks), :] = lines[
                    c, 0, pl.ds(j * toks + t, owners, stride=tokens), :
                ]
            out_ref[j, :, c * 128 : (c + 1) * 128] = lines[
                c, 1, j * size : (j + 1) * size, :
            ].astype(BF16)


def on_device(
    queries,
    cand_keys,
    candidate_values,
    cached_prompt_keys,
    cached_prompt_values,
    block_lists,
    out_weight,
):
    cands, toks, heads, head = queries.shape
    kv = cand_keys.shape[2]
    group = heads // kv
    blocks, block_tokens = cached_prompt_keys.shape[:2]
    ranges = lax.axis_size("ctx")
    depth = ranges // 4
    piece = cands * toks * heads
    per = toks * group
    pair = kv // 2
    vmem = pl.BlockSpec(memory_space=pltpu.VMEM)
    anywhere = pl.BlockSpec(memory_space=pl.ANY)
    tile_owners = min(ranges, 256 // per)
    rows = tile_owners * per
    unit_rows = cands * per + per
    most = min(blocks, cands * block_lists.shape[1] // ranges)
    entries = most + (cands - 1) * most // 2
    slots = ((entries + cands) // 2 + 1) // 2 * 2
    columns = out_weight.shape[1]
    tokens = cands * toks
    half = ranges * tokens // 2
    dma = pltpu.SemaphoreType.DMA
    semaphores = lambda slots: [dma, dma((slots, 2))]
    block = pltpu.VMEM((depth, 2, pair, unit_rows, head), BF16)
    sizes = (cands, toks, kv, group, head, tile_owners, slots)
    cache = (blocks, block_tokens * kv, head)
    return pl.pallas_call(
        functools.partial(fused_kernel, ranges, sizes),
        out_shape=jax.ShapeDtypeStruct((cands, ranges * toks // 2, columns), BF16),
        in_specs=[pl.BlockSpec(memory_space=pltpu.SMEM)] + [anywhere] * 7,
        out_specs=vmem,
        scratch_shapes=[
            pltpu.VMEM(block_lists.shape, jnp.int32),
            pltpu.VMEM(cand_keys.shape, BF16),
            pltpu.VMEM(candidate_values.shape, BF16),
            pltpu.VMEM((ranges, 2, cands, toks, heads // 2, head), BF16),
            pltpu.VMEM((2, *cache), BF16),
            pltpu.VMEM((block_tokens * kv, head), F32),
            pltpu.VMEM((2, kv, blocks, block_tokens, head), BF16),
            pltpu.SMEM((6, slots), jnp.int32),
            pltpu.VMEM((pair, cands, rows, head), BF16),
            pltpu.VMEM((2, kv, block_tokens, head), BF16),
            pltpu.VMEM((pair, slots, 2, rows, block_tokens), F32),
            pltpu.VMEM((pair, slots + 1, rows, block_tokens), F32),
            pltpu.VMEM((pair, slots + 1, rows, head), F32),
            pltpu.VMEM((pair, cands, rows, block_tokens), F32),
            pltpu.VMEM((pair, cands, rows, block_tokens), F32),
            pltpu.VMEM((pair, cands, rows, head), F32),
            pltpu.VMEM((ranges, 2, pair, unit_rows, head), BF16),
        ]
        + [block] * 6
        + [
            pltpu.VMEM((ranges, 2, piece // 2, head), BF16),
            pltpu.VMEM((piece, head), F32),
            pltpu.VMEM(out_weight.shape, BF16),
            pltpu.VMEM((2 * half, columns), F32),
            pltpu.VMEM((half, columns), BF16),
            pltpu.VMEM((half, columns), BF16),
            pltpu.VMEM((columns // 128, 2, half, 128), F32),
            dma((7,)),
            *semaphores(2 * depth),
            *semaphores(2 * depth + 1),
            *semaphores(2 * depth),
            dma((2,)),
        ],
        compiler_params=pltpu.CompilerParams(
            collective_id=0, has_side_effects=True, vmem_limit_bytes=60 * 1024 * 1024
        ),
        name="verify",
    )(
        block_lists,
        block_lists,
        queries,
        cand_keys,
        candidate_values,
        cached_prompt_keys.reshape(cache),
        cached_prompt_values.reshape(cache),
        out_weight,
    )


def solution(mesh):
    placed = (
        P("groups", "ctx", "tp", None),
        P("groups", "ctx", "tp", None),
        P("groups", "ctx", "tp", None),
        P(("groups", "ctx"), None, "tp", None),
        P(("groups", "ctx"), None, "tp", None),
        P("groups", None),
        P("tp", "ctx"),
    )
    return jax.shard_map(
        on_device, mesh=mesh, in_specs=placed, out_specs=P("groups", "tp", "ctx"), check_vma=False
    )
```

```python
import functools
import math

import jax
import jax.numpy as jnp
from jax import lax
from jax.experimental import pallas as pl
from jax.experimental.pallas import tpu as pltpu
from jax.sharding import PartitionSpec as P

NEGATIVE = -1e30
MESH = pl.DeviceIdType.MESH
F32, BF16 = jnp.float32, jnp.bfloat16


class Place:
    def __init__(self, ranges):
        self.me = lax.axis_index("ctx")
        self.depth = ranges // 4
        self.x, self.y, self.z = self.me % 2, (self.me // 2) % 2, self.me // 4
        self.beside_x = self.at(self.z, self.y, 1 - self.x)
        self.beside_y = self.at(self.z, 1 - self.y, self.x)

    def at(self, z, y, x):
        return z * 4 + y * 2 + x

    def shifted(self, d):
        return (self.z + d + self.depth) % self.depth

    def line(self, d):
        return self.at(self.shifted(d), self.y, self.x)


def greet(place):
    barrier = pltpu.get_barrier_semaphore()
    others = [place.line(d) for d in range(1, place.depth)]
    for other in others + [place.beside_x, place.beside_y]:
        pl.semaphore_signal(barrier, inc=1, device_id={"ctx": other}, device_id_type=MESH)
    pl.semaphore_signal(
        barrier, inc=1, device_id={"tp": 1 - lax.axis_index("tp")}, device_id_type=MESH
    )


def near_first(depth):
    order = []
    for step in range(1, depth // 2 + 1):
        order += [step] + ([depth - step] if depth - step != step else [])
    return order


def merge(pieces, combos, per, scale):
    full = combos * per
    stats = [load(full, per).astype(F32) for load in pieces]
    peak = functools.reduce(jnp.maximum, stats)
    low = lax.broadcasted_iota(jnp.int32, (per, 128), 1) < 64
    scales = [jnp.exp2((jnp.where(low, s - peak, 0.0)) * scale) for s in stats]
    total = sum(pltpu.roll(w, 64, 1) * s for w, s in zip(scales, stats))
    sums = []
    for c in range(combos):
        sums.append(
            sum(
                load(c * per, per).astype(F32) * w[:, c : c + 1]
                for load, w in zip(pieces, scales)
            )
        )
    return sums, jnp.where(low, peak, total), total


class Gather:
    def __init__(self, place, buf, send, recv):
        self.place, self.buf, self.send, self.recv = place, buf, send, recv
        self.z_of = [place.shifted(-d) for d in range(place.depth)]

    def go(self, piece, slot, half, target):
        pltpu.make_async_remote_copy(
            src_ref=piece,
            dst_ref=piece,
            send_sem=self.send,
            recv_sem=self.recv.at[slot, half],
            device_id={"ctx": target},
            device_id_type=MESH,
        ).start()

    def wait(self, count, slot, half):
        some = self.buf.at[pl.ds(0, count), half]
        pltpu.make_async_copy(some, some, self.recv.at[slot, half]).wait()

    def begin(self, half):
        place = self.place
        self.spread(0, half)
        for d in near_first(place.depth):
            self.go(self.buf.at[place.me, half], d, half, place.line(d))

    def spread(self, d, half):
        place = self.place
        owner = place.at(self.z_of[d], place.y, place.x)
        if d:
            self.wait(1, d, half)
        for target in (place.beside_x, place.beside_y):
            self.go(self.buf.at[owner, half], place.depth + d, half, target)

    def relay(self, d, half):
        place = self.place
        self.wait(2, place.depth + d, half)
        size = self.buf.shape[2] // 2
        from_x = place.at(self.z_of[d], place.y, 1 - place.x)
        from_y = place.at(self.z_of[d], 1 - place.y, place.x)
        self.go(self.buf.at[from_x, half, pl.ds(0, size)], 0, half, place.beside_y)
        self.go(self.buf.at[from_y, half, pl.ds(size, size)], 0, half, place.beside_x)

    def settle(self, half):
        self.wait(self.place.depth, 0, half)

    def finish(self):
        away = self.buf.at[pl.ds(0, self.buf.shape[0] - 1)]
        pltpu.make_async_copy(away, away, self.send).wait()


def run_all(steps):
    for step in steps:
        step()


def fused_kernel(
    ranges,
    sizes,
    lists_smem,
    lists_hbm,
    q_ref,
    own_k_hbm,
    own_v_hbm,
    k_ref,
    v_ref,
    weight_ref,
    out_ref,
    lists_ref,
    own_k_ref,
    own_v_ref,
    everyone,
    raw,
    wide,
    heads,
    plan,
    queries,
    own_blocks,
    scores,
    run,
    acc,
    peaks,
    own_sums,
    own_acc,
    parts_ref,
    from_diag,
    from_x,
    from_y,
    from_line,
    to_diag,
    to_line,
    gathered,
    ordered,
    weight,
    total,
    away,
    arrived,
    lines,
    in_sems,
    ask_send,
    ask_recv,
    red_send,
    red_recv,
    send,
    recv,
    tp_sems,
):
    cands, toks, kv, group, head, tile_owners, slots = sizes
    place = Place(ranges)
    depth = place.depth
    per = toks * group
    pair = kv // 2
    scale = head ** (-0.5) * math.log2(math.e)
    rows = tile_owners * per
    blocks, block_tokens = raw.shape[1], raw.shape[2] // kv
    greet(place)
    mine = [
        pltpu.make_async_copy(
            q_ref.at[:, :, pl.ds(half * pair * group, pair * group), :],
            everyone.at[place.me, half],
            in_sems.at[3],
        )
        for half in range(2)
    ]
    small = [(lists_hbm, lists_ref), (own_k_hbm, own_k_ref), (own_v_hbm, own_v_ref)]
    local = [
        pltpu.make_async_copy(src, dst, in_sems.at[4 + n]) for n, (src, dst) in enumerate(small)
    ]
    for one in mine + local:
        one.start()
    sources = (k_ref, v_ref)
    fetches = [pltpu.make_async_copy(sources[n], raw.at[n], in_sems.at[n]) for n in range(2)]
    for fetch in fetches:
        fetch.start()
    weight_fetch = pltpu.make_async_copy(weight_ref, weight, in_sems.at[2])
    whole = everyone.at[place.me]
    pltpu.make_async_copy(whole, whole, in_sems.at[3]).wait()
    pl.semaphore_wait(pltpu.get_barrier_semaphore(), depth + 2)

    ask = Gather(place, everyone, ask_send, ask_recv)
    near = near_first(depth)
    ask.begin(0)
    ask.begin(1)
    for one in local:
        one.wait()

    lowest = place.me * blocks
    listed = lists_smem.shape[1]
    below, count, start = [], [], [jnp.int32(0)]
    for j in range(cands):
        line = lists_ref[j : j + 1, :]
        below.append(jnp.sum((line < lowest).astype(jnp.int32)))
        count.append(jnp.sum((line < lowest + blocks).astype(jnp.int32)) - below[j])
        start.append(jnp.minimum(start[j] + (count[j] + 1) // 2, slots))

    def plan_slot(i, carry):
        cand, begun, under, many = jnp.int32(0), jnp.int32(0), below[0], count[0]
        for j in range(1, cands):
            here = i >= start[j]
            cand = jnp.where(here, j, cand)
            begun = jnp.where(here, start[j], begun)
            under = jnp.where(here, below[j], under)
            many = jnp.where(here, count[j], many)
        offset = 2 * (i - begun)
        plan[0, i] = cand
        for n in range(2):
            entry = jnp.minimum(under + offset + n, listed - 1)
            block = lists_smem[cand, entry] - lowest
            plan[1 + n, i] = jnp.minimum(jnp.maximum(block, 0), blocks - 1)
            plan[3 + n, i] = (offset + n < many).astype(jnp.int32)
        plan[5, i] = (offset == 0).astype(jnp.int32)
        return carry

    lax.fori_loop(0, slots, plan_slot, 0)

    def sort_heads(n, first, last):
        def one(b, carry):
            wide[...] = raw[n, b].astype(F32)
            for h in range(kv):
                heads[n, h, b] = wide[pl.ds(h, block_tokens, stride=kv), :].astype(BF16)
            return carry

        lax.fori_loop(first, last, one, 0)

    key_row = lax.broadcasted_iota(jnp.int32, (block_tokens, head), 0)

    def own_rows():
        for n, ref in enumerate((own_k_ref, own_v_ref)):
            mine = [ref[j].astype(F32) for j in range(cands)]
            for h in range(kv):
                block = jnp.zeros((block_tokens, head), F32)
                for j in range(cands):
                    for t in range(toks):
                        block = jnp.where(
                            key_row == j * toks + t, mine[j][t, h : h + 1, :], block
                        )
                own_blocks[n, h] = block.astype(BF16)

    def sort_step(n, part):
        def step():
            if part == 0:
                fetches[n].wait()
            sort_heads(n, part * (blocks // 4), (part + 1) * (blocks // 4))

        return step

    part = functools.partial

    def each(step, ds, half):
        return [part(step, d, half) for d in ds]

    come = near
    run_all([sort_step(0, i) for i in range(4)])
    ask.relay(0, 0)
    run_all(each(ask.spread, come[:1], 0) + [sort_step(1, 0)])
    weight_fetch.start()
    run_all(each(ask.spread, come[1:], 0) + [sort_step(1, 1)])
    ask.relay(0, 1)
    run_all(each(ask.spread, come, 1) + [sort_step(1, 2), sort_step(1, 3), own_rows])
    run_all(each(ask.relay, come, 0))

    nt = (((1,), (1,)), ((), ()))
    row = lax.broadcasted_iota(jnp.int32, (rows, block_tokens), 0)
    lane = lax.broadcasted_iota(jnp.int32, (rows, block_tokens), 1)
    unroll = max(n for n in range(1, 12) if slots % n == 0)

    def attend(half, tile, between):
        owners = pl.ds(tile * tile_owners, tile_owners)
        query_pos = tile * tile_owners * toks + row // group

        def own_seen(j):
            t = lane - j * toks
            return (t >= 0) & (t < toks) & (place.me * toks + t <= query_pos)

        for hh in range(pair):
            run[hh, 0] = jnp.full((rows, block_tokens), NEGATIVE, F32)
            acc[hh, 0] = jnp.zeros((rows, head), F32)
            for j in range(cands):
                q = everyone[owners, half, j, :, hh * group : (hh + 1) * group, :].astype(F32)
                queries[hh, j] = q.reshape(rows, head).astype(BF16)

        def first_pass(it, carry):
            for u in range(unroll):
                i = it * unroll + u
                cand, fresh = plan[0, i], plan[5, i] > 0
                for hh in range(pair):
                    h = half * pair + hh
                    keys = jnp.concatenate(
                        [heads[0, h, plan[1, i]], heads[0, h, plan[2, i]]], axis=0
                    )
                    s = lax.dot_general(queries[hh, cand], keys, nt, preferred_element_type=F32)
                    top = jnp.where(fresh, NEGATIVE, run[hh, i])
                    for n in range(2):
                        one = s[:, n * block_tokens : (n + 1) * block_tokens]
                        one = jnp.where(plan[3 + n, i] > 0, one, NEGATIVE)
                        scores[hh, i, n] = one
                        top = jnp.maximum(top, one)
                    run[hh, i + 1] = top
            return carry

        lax.fori_loop(0, slots // unroll, first_pass, 0)
        between[0]()
        for hh in range(pair):
            h = half * pair + hh
            for j in range(cands):
                seen = own_seen(j)
                own = lax.dot_general(
                    queries[hh, j], own_blocks[0, h], nt, preferred_element_type=F32
                )
                own = jnp.where(seen, own, NEGATIVE)
                top = jnp.where(count[j] > 0, run[hh, start[j + 1]], NEGATIVE)
                top = jnp.maximum(top, own)
                peak = jnp.max(top, axis=1, keepdims=True).astype(BF16).astype(F32)
                p = jnp.where(seen, jnp.exp2((own - peak) * scale), 0.0)
                own_sums[hh, j] = p
                own_acc[hh, j] = jnp.dot(
                    p.astype(BF16), own_blocks[1, h], preferred_element_type=F32
                )
                peaks[hh, j] = jnp.broadcast_to(peak, (rows, block_tokens))
        between[1]()

        def second_pass(it, carry):
            for u in range(unroll):
                i = it * unroll + u
                cand, fresh = plan[0, i], plan[5, i] > 0
                for hh in range(pair):
                    h = half * pair + hh
                    peak = peaks[hh, cand]
                    p = [jnp.exp2((scores[hh, i, n] - peak) * scale) for n in range(2)]
                    run[hh, i + 1] = jnp.where(fresh, 0.0, run[hh, i]) + (p[0] + p[1])
                    values = jnp.concatenate(
                        [heads[1, h, plan[1, i]], heads[1, h, plan[2, i]]], axis=0
                    )
                    weights = jnp.concatenate([one.astype(BF16) for one in p], axis=1)
                    acc[hh, i + 1] = jnp.where(fresh, 0.0, acc[hh, i]) + jnp.dot(
                        weights, values, preferred_element_type=F32
                    )
            return carry

        middle = slots // unroll // 2
        lax.fori_loop(0, middle, second_pass, 0)
        between[2]()
        lax.fori_loop(middle, slots // unroll, second_pass, 0)
        between[3]()
        lanes = lax.broadcasted_iota(jnp.int32, (rows, 128), 1)
        for hh in range(pair):
            stats = jnp.zeros((rows, 128), F32)
            for j in range(cands):
                last, some = start[j + 1], count[j] > 0
                sums = jnp.where(some, run[hh, last], 0.0) + own_sums[hh, j]
                found = jnp.where(some, acc[hh, last], 0.0) + own_acc[hh, j]
                stats = jnp.where(lanes == j, peaks[hh, j], stats)
                stats = jnp.where(
                    lanes == 64 + j, jnp.sum(sums, axis=1, keepdims=True), stats
                )
                parts_ref[owners, half, hh, j * per : (j + 1) * per, :] = found.reshape(
                    tile_owners, per, head
                ).astype(BF16)
            parts_ref[owners, half, hh, cands * per : (cands + 1) * per, :] = stats.reshape(
                tile_owners, per, 128
            ).astype(BF16)

    def go(slot, half, src, dst, target):
        pltpu.make_async_remote_copy(
            src_ref=src,
            dst_ref=dst,
            send_sem=red_send,
            recv_sem=red_recv.at[slot, half],
            device_id={"ctx": target},
            device_id_type=MESH,
        ).start()

    def arrive(slot, half, some):
        pltpu.make_async_copy(some, some, red_recv.at[slot, half]).wait()

    def owner(d, flip_y, flip_x):
        y = 1 - place.y if flip_y else place.y
        x = 1 - place.x if flip_x else place.x
        return place.at(place.shifted(d), y, x)

    def loader(ref, *index):
        return lambda start, size: ref[(*index, pl.ds(start, size), slice(None))]

    def put(dst, index, sums, stats):
        for c in range(cands):
            dst[(*index, slice(c * per, (c + 1) * per), slice(None))] = sums[c].astype(BF16)
        dst[(*index, slice(cands * per, (cands + 1) * per), slice(None))] = stats.astype(BF16)

    def hand_over(d, half):
        across = owner(d, 1, 1)
        for u, target in enumerate((place.beside_x, place.beside_y)):
            go(d, half, parts_ref.at[across, half, u], from_diag.at[d, half, u], target)

    def hand_beside(d, half):
        x_owner, y_owner = owner(d, 0, 1), owner(d, 1, 0)
        slot = depth + d
        go(slot, half, parts_ref.at[x_owner, half, 0], from_x.at[d, half, 0], place.beside_x)
        go(slot, half, parts_ref.at[y_owner, half, 1], from_y.at[d, half, 1], place.beside_y)

    def pass_on(d, half):
        arrive(d, half, from_diag.at[d, half])
        for u in range(2):
            mine = owner(d, 1, 0) if u == 0 else owner(d, 0, 1)
            pieces = (loader(parts_ref, mine, half, u), loader(from_diag, d, half, u))
            sums, stats, _ = merge(pieces, cands, per, scale)
            put(to_diag, (d, half, u), sums, stats)
            into, target = (from_y, place.beside_y) if u == 0 else (from_x, place.beside_x)
            go(depth + d, half, to_diag.at[d, half, u], into.at[d, half, u], target)

    def plane(d, half):
        arrive(depth + d, half, parts_ref.at[pl.ds(0, 2), half])
        for u in range(2):
            pieces = (
                loader(parts_ref, owner(d, 0, 0), half, u),
                loader(from_x, d, half, u),
                loader(from_y, d, half, u),
            )
            sums, stats, _ = merge(pieces, cands, per, scale)
            put(to_line, (d, half, u), sums, stats)
        if d:
            go(2 * depth, half, to_line.at[d, half], from_line.at[d, half], place.line(d))

    far = near[::-1] + [0]

    def hand_all(half):
        for d in far:
            hand_over(d, half)
        for d in far:
            hand_beside(d, half)

    tokens = cands * toks

    def conclude(half):
        arrive(2 * depth, half, from_line.at[pl.ds(0, depth - 1), half])
        for u in range(2):
            lines_in = [loader(from_line, d, half, u) for d in range(1, depth)]
            sums, _, denominator = merge(
                [loader(to_line, 0, half, u)] + lines_in, cands, per, scale
            )
            inverse = 1.0 / pltpu.roll(denominator, 64, 1)
            for c in range(cands):
                at = ((half * 2 + u) * cands + c) * per
                ordered[at : at + per, :] = sums[c] * inverse[:, c : c + 1]
        for hh in range(pair):
            h = half * pair + hh
            block = [
                ordered[pl.ds(h * tokens * group + g, tokens, stride=group), :]
                for g in range(group)
            ]
            at = hh * tokens * group
            gathered[place.me, half, at : at + tokens * group, :] = jnp.concatenate(
                block, axis=0
            ).astype(BF16)

    tell = Gather(place, gathered, send, recv)

    count_half = kv * group // 2
    deep = math.gcd(count_half, 8)

    def project(i, carry):
        at = pl.multiple_of((i * deep) % count_half * tokens, deep * tokens)
        some = gathered[:, i * deep // count_half, pl.ds(at, deep * tokens), :].astype(F32)
        inputs = [
            some[:, n * tokens : (n + 1) * tokens, :].reshape(ranges * tokens, head).astype(BF16)
            for n in range(deep)
        ]
        total[...] += jnp.dot(
            jnp.concatenate(inputs, axis=1),
            weight[pl.ds(pl.multiple_of(i * deep * head, deep * head), deep * head), :],
            preferred_element_type=F32,
        )
        return carry

    tiles = ranges // tile_owners

    def attend_all(half, *steps):
        for tile in range(tiles):
            last = tile == tiles - 1
            attend(half, tile, [part(run_all, some if last else []) for some in steps])

    ask.settle(0)
    attend_all(0, each(ask.relay, come, 1), [], [], [])
    hand_all(0)
    ask.settle(1)
    early = depth // 2
    attend_all(
        1,
        each(pass_on, far[:early], 0),
        each(pass_on, far[early:], 0),
        [],
        each(plane, far[:early], 0),
    )
    hand_all(1)
    run_all(each(plane, far[early:], 0))
    run_all(each(pass_on, far, 1))
    conclude(0)
    run_all(each(plane, far, 1))
    tell.begin(0)
    conclude(1)
    tell.begin(1)
    total[...] = jnp.zeros_like(total)
    weight_fetch.wait()
    run_all(each(tell.relay, [0], 0) + each(tell.spread, come, 0))
    run_all(each(tell.relay, [0], 1) + each(tell.spread, come, 1))
    run_all(each(tell.relay, come, 0) + each(tell.relay, come, 1))
    steps = count_half // deep
    tell.settle(0)
    lax.fori_loop(0, steps, project, 0)
    tell.settle(1)
    lax.fori_loop(steps, 2 * steps, project, 0)
    half_rows = ranges * tokens // 2
    tp = lax.axis_index("tp")
    away[...] = total[
        pl.ds(pl.multiple_of((1 - tp) * half_rows, half_rows), half_rows), :
    ].astype(BF16)
    swap = pltpu.make_async_remote_copy(
        src_ref=away,
        dst_ref=arrived,
        send_sem=tp_sems.at[0],
        recv_sem=tp_sems.at[1],
        device_id={"tp": 1 - tp},
        device_id_type=MESH,
    )
    swap.start()
    ask.finish()
    tell.finish()
    handed = parts_ref.at[pl.ds(0, ranges - 1)]
    pltpu.make_async_copy(handed, handed, red_send).wait()
    swap.wait()
    mine = total[pl.ds(pl.multiple_of(tp * half_rows, half_rows), half_rows), :]
    columns = total.shape[1]
    joined = mine + arrived[...].astype(F32)
    owners, size = ranges // 2, ranges // 2 * toks
    for c in range(columns // 128):
        lines[c, 0] = joined[:, c * 128 : (c + 1) * 128]
        for j in range(cands):
            for t in range(toks):
                lines[c, 1, pl.ds(j * size + t, owners, stride=toks), :] = lines[
                    c, 0, pl.ds(j * toks + t, owners, stride=tokens), :
                ]
            out_ref[j, :, c * 128 : (c + 1) * 128] = lines[
                c, 1, j * size : (j + 1) * size, :
            ].astype(BF16)


def on_device(
    queries,
    cand_keys,
    candidate_values,
    cached_prompt_keys,
    cached_prompt_values,
    block_lists,
    out_weight,
):
    cands, toks, heads, head = queries.shape
    kv = cand_keys.shape[2]
    group = heads // kv
    blocks, block_tokens = cached_prompt_keys.shape[:2]
    ranges = lax.axis_size("ctx")
    depth = ranges // 4
    piece = cands * toks * heads
    per = toks * group
    pair = kv // 2
    vmem = pl.BlockSpec(memory_space=pltpu.VMEM)
    anywhere = pl.BlockSpec(memory_space=pl.ANY)
    tile_owners = min(ranges, 256 // per)
    rows = tile_owners * per
    unit_rows = cands * per + per
    most = min(blocks, cands * block_lists.shape[1] // ranges)
    entries = most + (cands - 1) * most // 2
    slots = ((entries + cands) // 2 + 1) // 2 * 2
    columns = out_weight.shape[1]
    tokens = cands * toks
    half = ranges * tokens // 2
    dma = pltpu.SemaphoreType.DMA
    semaphores = lambda slots: [dma, dma((slots, 2))]
    block = pltpu.VMEM((depth, 2, pair, unit_rows, head), BF16)
    sizes = (cands, toks, kv, group, head, tile_owners, slots)
    cache = (blocks, block_tokens * kv, head)
    return pl.pallas_call(
        functools.partial(fused_kernel, ranges, sizes),
        out_shape=jax.ShapeDtypeStruct((cands, ranges * toks // 2, columns), BF16),
        in_specs=[pl.BlockSpec(memory_space=pltpu.SMEM)] + [anywhere] * 7,
        out_specs=vmem,
        scratch_shapes=[
            pltpu.VMEM(block_lists.shape, jnp.int32),
            pltpu.VMEM(cand_keys.shape, BF16),
            pltpu.VMEM(candidate_values.shape, BF16),
            pltpu.VMEM((ranges, 2, cands, toks, heads // 2, head), BF16),
            pltpu.VMEM((2, *cache), BF16),
            pltpu.VMEM((block_tokens * kv, head), F32),
            pltpu.VMEM((2, kv, blocks, block_tokens, head), BF16),
            pltpu.SMEM((6, slots), jnp.int32),
            pltpu.VMEM((pair, cands, rows, head), BF16),
            pltpu.VMEM((2, kv, block_tokens, head), BF16),
            pltpu.VMEM((pair, slots, 2, rows, block_tokens), F32),
            pltpu.VMEM((pair, slots + 1, rows, block_tokens), F32),
            pltpu.VMEM((pair, slots + 1, rows, head), F32),
            pltpu.VMEM((pair, cands, rows, block_tokens), F32),
            pltpu.VMEM((pair, cands, rows, block_tokens), F32),
            pltpu.VMEM((pair, cands, rows, head), F32),
            pltpu.VMEM((ranges, 2, pair, unit_rows, head), BF16),
        ]
        + [block] * 6
        + [
            pltpu.VMEM((ranges, 2, piece // 2, head), BF16),
            pltpu.VMEM((piece, head), F32),
            pltpu.VMEM(out_weight.shape, BF16),
            pltpu.VMEM((2 * half, columns), F32),
            pltpu.VMEM((half, columns), BF16),
            pltpu.VMEM((half, columns), BF16),
            pltpu.VMEM((columns // 128, 2, half, 128), F32),
            dma((7,)),
            *semaphores(2 * depth),
            *semaphores(2 * depth + 1),
            *semaphores(2 * depth),
            dma((2,)),
        ],
        compiler_params=pltpu.CompilerParams(
            collective_id=0, has_side_effects=True, vmem_limit_bytes=60 * 1024 * 1024
        ),
        name="verify",
    )(
        block_lists,
        block_lists,
        queries,
        cand_keys,
        candidate_values,
        cached_prompt_keys.reshape(cache),
        cached_prompt_values.reshape(cache),
        out_weight,
    )


def solution(mesh):
    placed = (
        P("groups", "ctx", "tp", None),
        P("groups", "ctx", "tp", None),
        P("groups", "ctx", "tp", None),
        P(("groups", "ctx"), None, "tp", None),
        P(("groups", "ctx"), None, "tp", None),
        P("groups", None),
        P("tp", "ctx"),
    )
    return jax.shard_map(
        on_device, mesh=mesh, in_specs=placed, out_specs=P("groups", "tp", "ctx"), check_vma=False
    )
```
